256 devices in a mesh: frames: 4 (over z_hi), states: 64 (over z_lo, y, x, core).
Axes of the slice: x: 4, y: 4, z: 8 (z_hi: 4, z_lo: 2; z = z_hi * 2 + z_lo), core: 2. Of those that a mesh axis runs over, the one named last changes fastest.
Arguments:
- features: bfloat16 [16384, 1024], P('states', 'frames'), may hold values from -10 to 10
- state_ids: int32 [16384, 32], P('states'), may hold values from 0 to 6143, as said below
- weights: float32 [16384, 32], P('states'), may hold values from 0.05 to 1
Outputs:
- means: bfloat16 [6144, 1024], P(None, 'frames')
- precisions: bfloat16 [6144, 1024], P(None, 'frames')
- frame_score: float32 [16384], P('states')
The draws below stay inside these ranges and needn't reach their ends.
Inputs may be any that keep to these rules, and one draw needn't show every extreme that they name: `state_ids`: each row names 32 different states; every state is named by some row.
All inputs are finite; a program needn't handle non-finite values.
Results may differ from the reference program's by a relative error of at most 0.0034.
Values may be sent and summed in bfloat16 or wider, within the bound.
A program may use at most 128 MiB of HBM per device.

```python
import math
import jax
import jax.numpy as jnp
from jax import lax

D = 1024
TOPK = 32
ALL_STATES = 6144
ALL_FRAMES = 16384


def frame_layout(key):
    base_key = jax.random.fold_in(key, 101)
    layout_keys = jax.random.split(base_key, 6)
    cluster_count = ALL_STATES // (2 * TOPK)
    order = jax.random.permutation(layout_keys[0], ALL_FRAMES).astype(jnp.int32)
    home = order % cluster_count
    rank = order // cluster_count
    return (home, rank, layout_keys)


def draw_state_ids(key, part):
    home, rank, layout_keys = frame_layout(key)
    group = 2 * TOPK
    cluster_count = ALL_STATES // group
    outside = TOPK // 8
    inside = TOPK - outside
    state_order = jax.random.permutation(layout_keys[1], ALL_STATES).astype(jnp.int32)
    position = jnp.arange(group, dtype=jnp.int32)[None, :]
    random_score = jax.random.randint(layout_keys[2], (ALL_FRAMES, group), 0, 2 ** 20, dtype=jnp.int32) * group + position
    forced_score = (position - rank[:, None] * inside) % group
    score = jnp.where(rank[:, None] < 3, forced_score, random_score)
    picked = jnp.argsort(score, axis=1)[:, :inside].astype(jnp.int32)
    chosen = home[:, None] * group + picked
    if outside > 0:
        offset = jax.random.randint(layout_keys[3], (ALL_FRAMES,), 1, cluster_count, dtype=jnp.int32)
        neighbour = (home + offset) % cluster_count
        other_score = jax.random.randint(layout_keys[4], (ALL_FRAMES, group), 0, 2 ** 20, dtype=jnp.int32) * group + position
        extra = jnp.argsort(other_score, axis=1)[:, :outside].astype(jnp.int32)
        chosen = jnp.concatenate([chosen, neighbour[:, None] * group + extra], axis=1)
    state_list = state_order[chosen]
    column_score = jax.random.randint(layout_keys[5], (ALL_FRAMES, TOPK), 0, 2 ** 20, dtype=jnp.int32) * TOPK + jnp.arange(TOPK, dtype=jnp.int32)[None, :]
    column_order = jnp.argsort(column_score, axis=1).astype(jnp.int32)
    return jnp.take_along_axis(state_list, column_order, axis=1).astype(jnp.int32)


def draw_features(key, part):
    home, rank, layout_keys = frame_layout(key)
    cluster_count = ALL_STATES // (2 * TOPK)
    feature_keys = jax.random.split(jax.random.fold_in(key, 17), 5)
    scales = jnp.exp(jax.random.uniform(feature_keys[0], (D,), jnp.float32, math.log(0.2), math.log(2.0)))
    offsets = jax.random.uniform(feature_keys[1], (D,), jnp.float32, -1.5, 1.5)
    cluster_shift = jax.random.uniform(feature_keys[3], (cluster_count, D), jnp.float32, -1.0, 1.0)
    cluster_scale = jnp.exp(jax.random.uniform(feature_keys[4], (cluster_count,), jnp.float32, math.log(0.5), math.log(2.0)))
    noise = jnp.clip(jax.random.normal(feature_keys[2], (ALL_FRAMES, D), jnp.float32), -4.0, 4.0)
    centre = offsets[None, :] + 1.5 * cluster_shift[home]
    spread = scales[None, :] * cluster_scale[home][:, None]
    return jnp.clip(centre + spread * noise, -10.0, 10.0).astype(jnp.bfloat16)


def level_of(stream_key, extent, cuts, low, largest):
    def one(dim, blocks):
        heights = jax.random.uniform(jax.random.fold_in(jax.random.fold_in(stream_key, 6), dim), (blocks,), jnp.float32, low / len(cuts), largest / len(cuts))
        return jnp.repeat(jnp.exp(heights), extent[dim] // blocks).reshape((-1,) + (1,) * (len(extent) - dim - 1))

    gain = one(*cuts[0])
    for cut in cuts[1:]:
        gain = gain * one(*cut)
    return gain


def setup_inputs(seed: int = 0) -> dict:
    key_of = jax.random.split(jax.random.key(seed), 4)
    features = draw_features(jax.random.fold_in(key_of[3], 71), 0)
    state_ids = draw_state_ids(jax.random.fold_in(key_of[3], 71), 0)
    weights = jnp.clip(jnp.exp(math.log(1.0) - 2.9957323 * jax.random.uniform(key_of[2], (ALL_FRAMES, TOPK), jnp.float32) ** level_of(key_of[2], (ALL_FRAMES, TOPK), ((0, 64),), -0.2, 0.2)), 0.05, 1.0)
    return dict(features=features, state_ids=state_ids, weights=weights)


variance_floor = 0.25


def reference(features, state_ids, weights):
    rounded = lax.optimization_barrier(weights.astype(jnp.bfloat16)).astype(jnp.float32)
    values = features.astype(jnp.float32)
    squares = lax.optimization_barrier((values * values).astype(jnp.bfloat16)).astype(jnp.float32)
    first = jnp.zeros((ALL_STATES, D), jnp.float32)
    second = jnp.zeros((ALL_STATES, D), jnp.float32)
    occupancy = jnp.zeros((ALL_STATES,), jnp.float32)
    for column in range(TOPK):
        chosen = state_ids[:, column]
        weight_col = rounded[:, column]
        first = first.at[chosen].add(weight_col[:, None] * values)
        second = second.at[chosen].add(weight_col[:, None] * squares)
        occupancy = occupancy.at[chosen].add(weight_col)
    mean_value = first / occupancy[:, None]
    variance = jnp.maximum(second / occupancy[:, None] - mean_value * mean_value, variance_floor)
    means = mean_value.astype(jnp.bfloat16)
    precisions = (1.0 / variance).astype(jnp.bfloat16)
    mean_f = means.astype(jnp.float32)
    prec_f = precisions.astype(jnp.float32)
    product = lax.optimization_barrier((mean_f * prec_f).astype(jnp.bfloat16)).astype(jnp.float32)
    constant = jnp.sum(mean_f * product - jnp.log(prec_f), axis=1)
    quadratic = jnp.zeros((ALL_FRAMES,), jnp.float32)
    for column in range(TOPK):
        chosen = state_ids[:, column]
        likely = jnp.sum(squares * prec_f[chosen] - 2.0 * values * product[chosen], axis=1) + constant[chosen]
        quadratic = quadratic + rounded[:, column] * likely
    frame_score = -0.5 * quadratic / (D * jnp.sum(rounded, axis=1))
    return means, precisions, frame_score
```

```python
import jax
import jax.numpy as jnp
from jax import lax
from jax.experimental import pallas as pl
from jax.experimental.pallas import tpu as pltpu
from jax.sharding import PartitionSpec as P

MESH = pl.DeviceIdType.MESH
F32, BF16, I16, I32 = jnp.float32, jnp.bfloat16, jnp.int16, jnp.int32
D = 1024
W = 256
ROWS = 96
OWN = 48
FLOOR = 0.25


def msg(k, j):
    return k * (k + 1) // 2 + j + 1


def flip(s, k):
    return s + 2**k * (1 - 2 * ((s // 2**k) % 2))


def sibling(s, j):
    if j < 0:
        return s, 1
    b = s // 2**j
    return (b + 1 - 2 * (b % 2)) * 2**j, 2**j


def rev4(s):
    return (s % 2) * 8 + ((s // 2) % 2) * 4 + ((s // 4) % 2) * 2 + s // 8


class Flood:
    def __init__(self, views, ssem, rsem, slot, slot_other, partners, core, c):
        self.views, self.ssem, self.rsem = views, ssem, rsem
        self.slot, self.slot_other, self.partners, self.core, self.c = slot, slot_other, partners, core, c

    def _copies(self, region, block, i, device):
        out = []
        for a, view in enumerate(self.views):
            ref = view(region, *block)
            out.append(
                pltpu.make_async_remote_copy(
                    src_ref=ref, dst_ref=ref, send_sem=self.ssem.at[i, a], recv_sem=self.rsem.at[i, a],
                    device_id={"states": device}, device_id_type=MESH,
                )
            )
        return out

    def _out(self, k, j):
        return self._copies(self.c, sibling(self.slot, j), msg(k, j), self.partners[k])

    def _in(self, k, j):
        return self._copies(self.c, sibling(flip(self.slot, k), j), msg(k, j), self.partners[k])

    def _core_out(self, k, j):
        s = self.slot if k < 0 else flip(self.slot, k)
        return self._copies(self.c, sibling(s, j), 10 if k < 0 else 11 + msg(k, j), self.core)

    def _core_in(self, k, j):
        s = self.slot_other if k < 0 else flip(self.slot_other, k)
        return self._copies(1 - self.c, sibling(s, j), 10 if k < 0 else 11 + msg(k, j), self.core)

    def start(self):
        for k in range(4):
            for cp in self._out(k, -1):
                cp.start()
        for cp in self._core_out(-1, -1):
            cp.start()

    def arrive(self, k):
        for j in range(-1, k):
            for cp in self._in(k, j):
                cp.wait_recv()
            for cp in self._core_out(k, j):
                cp.start()
        for later in range(k + 1, 4):
            for cp in self._out(later, k):
                cp.start()

    def arrive_core(self, k):
        for j in range(-1, k) if k >= 0 else (-1,):
            for cp in self._core_in(k, j):
                cp.wait_recv()

    def finish(self):
        for k in range(4):
            for j in range(-1, k):
                for cp in self._out(k, j):
                    cp.wait_send()
                for cp in self._core_out(k, j):
                    cp.wait_send()
        for cp in self._core_out(-1, -1):
            cp.wait_send()


def kernel(
    x_ref, ids_ref, w_ref, om_ref, op_ref, score_ref,
    xs, sq, g, post, acc, racc, qb, rq, q8, q4, q2, q1, r8, r4, r2, r1, rh,
    g_s, g_r, x_s, x_r, o_s, o_r, z_s, z_r, q_s, q_r, h_s, h_r,
):
    me = lax.axis_index("states")
    hi = lax.axis_index("frames")
    c = me % 2
    x = (me // 2) % 4
    y = (me // 8) % 4
    z = me // 32

    def device(z, y, x, c):
        return ((z * 4 + y) * 4 + x) * 2 + c

    p = x + c * (y - x)
    q = y + c * (x - y)

    def at(p2, q2):
        return device(z, q2 + c * (p2 - q2), p2 + c * (q2 - p2), c)

    v0, v1, v2, v3 = (p + p // 2) % 2, p // 2, (q + q // 2) % 2, q // 2
    near = [at(p + 1 - 2 * (p % 2), q), at(3 - p, q), at(p, q + 1 - 2 * (q % 2)), at(p, 3 - q)]
    core = device(z, y, x, 1 - c)
    up = device(1 - z, y, x, c)
    slot = (v0 + 2 * v1 + 4 * v2 + 8 * v3, v3 + 2 * v2 + 4 * v1 + 8 * v0)
    other = (v2 + 2 * v3 + 4 * v0 + 8 * v1, v1 + 2 * v0 + 4 * v3 + 8 * v2)

    barrier = pltpu.get_barrier_semaphore()
    for d in near + [core, up]:
        pl.semaphore_signal(barrier, inc=1, device_id={"states": d}, device_id_type=MESH)
    for d in range(1, 4):
        pl.semaphore_signal(barrier, inc=1, device_id={"frames": (hi + d) % 4}, device_id_type=MESH)

    codes = jnp.transpose(ids_ref[...])
    w_t = jnp.transpose(w_ref[...]).astype(BF16).astype(F32)
    g[c, slot[0], 0:32, :] = codes.astype(I16)
    g[c, slot[0], 32:64, :] = (w_t * 4096.0).astype(I32).astype(I16)
    for f in range(2):
        xs[f, c, pl.ds(pl.multiple_of(slot[f] * 128, 128), 128), :] = x_ref[f * 128 : (f + 1) * 128, :]
    acc[...] = jnp.zeros_like(acc)
    pl.semaphore_wait(barrier, 9)

    gf = Flood([lambda r, s, n: g.at[r, pl.ds(s, n)]], g_s, g_r, slot[0], other[0], near, core, c)

    def x_view(f):
        return lambda r, s, n: xs.at[f, r, pl.ds(pl.multiple_of(s * 128, 128), n * 128)]

    orders = (near, near[::-1])
    xf = [Flood([x_view(f)], x_s.at[f], x_r.at[f], slot[f], other[f], orders[f], core, c) for f in range(2)]
    gf.start()
    for f in range(2):
        xf[f].start()

    base = [pl.multiple_of(((c * 2 + part) * 16 + slot[part]) * ROWS, ROWS) for part in range(2)]
    iota = lax.broadcasted_iota(I32, (ROWS, 128), 0)
    rows = jnp.concatenate([(iota + base[0]).astype(I16), (iota + base[1]).astype(I16)], axis=0)

    def build_one(ch, s):
        ids = g[ch, s, 0:32, :].astype(I32)
        wv = g[ch, s, 32:64, :].astype(I32).astype(F32) * (1.0 / 4096.0)
        for f in range(2):
            lanes = slice(f * 128, (f + 1) * 128)
            block = jnp.zeros((2 * ROWS, 128), BF16)
            for j in range(32):
                idj = jnp.broadcast_to(ids[j : j + 1, lanes].astype(I16), (2 * ROWS, 128))
                wj = jnp.broadcast_to(wv[j : j + 1, lanes].astype(BF16), (2 * ROWS, 128))
                block = jnp.where(rows == idj, wj, block)
            col = pl.multiple_of((s if f == 0 else rev4(s)) * 128, 128)
            post[f, ch, :, pl.ds(col, 128)] = block
            acc[:, 512:640] += block.astype(F32)

    def build(ch, start, n):
        if n == 1:
            build_one(ch, start)
        else:
            @pl.loop(0, n)
            def _(i):
                build_one(ch, start + i)

    def moments(f, ch, start, n):
        r = pl.ds(pl.multiple_of(start * 128, 128), n * 128)
        xv = xs[f, ch, r, :]
        xw = xv.astype(F32)
        sv = (xw * xw).astype(BF16)
        sq[f, ch, r, :] = sv
        pv = post[f, ch, :, r]
        acc[:, 0:256] += jnp.dot(pv, xv, preferred_element_type=F32)
        acc[:, 256:512] += jnp.dot(pv, sv, preferred_element_type=F32)

    def x_step(k):
        for f in range(2):
            xf[f].arrive(k)

    def x_core(k):
        for f in range(2):
            xf[f].arrive_core(k)

    build(c, slot[0], 1)
    gf.arrive_core(-1)
    build(1 - c, other[0], 1)
    gf.arrive(0)
    build(c, *sibling(slot[0], 0))
    gf.arrive_core(0)
    build(1 - c, *sibling(other[0], 0))
    gf.arrive(1)
    x_step(0)
    build(c, *sibling(slot[0], 1))
    gf.arrive_core(1)
    build(1 - c, *sibling(other[0], 1))
    gf.arrive(2)
    x_step(1)
    build(c, *sibling(slot[0], 2))
    gf.arrive_core(2)
    build(1 - c, *sibling(other[0], 2))
    gf.arrive(3)
    x_step(2)
    build(c, *sibling(slot[0], 3))
    gf.arrive_core(3)
    build(1 - c, *sibling(other[0], 3))
    for k in range(-1, 3):
        x_core(k)
        for f in range(2):
            moments(f, c, *sibling(slot[f], k))
            moments(f, 1 - c, *sibling(other[f], k))
    x_step(3)
    for f in range(2):
        moments(f, c, *sibling(slot[f], 3))
    x_core(3)
    for f in range(2):
        moments(f, 1 - c, *sibling(other[f], 3))

    def acc_copy(part):
        return pltpu.make_async_remote_copy(
            src_ref=acc.at[pl.ds(pl.multiple_of(part * ROWS + (1 - z) * OWN, 8), OWN)], dst_ref=racc.at[part],
            send_sem=z_s.at[part], recv_sem=z_r.at[part], device_id={"states": up}, device_id_type=MESH,
        )

    def own_rows(part, zz):
        return pl.ds(pl.multiple_of(base[part] + zz * OWN, 16), OWN)

    def up_copies(part, zz):
        return [
            pltpu.make_async_remote_copy(
                src_ref=ref.at[own_rows(part, zz)], dst_ref=ref.at[own_rows(part, zz)],
                send_sem=z_s.at[2 + part * 2 + a], recv_sem=z_r.at[2 + part * 2 + a],
                device_id={"states": up}, device_id_type=MESH,
            )
            for a, ref in enumerate((om_ref, op_ref))
        ]

    for part in range(2):
        acc_copy(part).start()
    for part in range(2):
        acc_copy(part).wait_recv()
        total = acc[pl.ds(pl.multiple_of(part * ROWS + z * OWN, 8), OWN), :] + racc[part]
        inv_count = jnp.sum(total[:, 512:640], axis=1, keepdims=True)
        mean = total[:, 0:256] / inv_count
        var = jnp.maximum(total[:, 256:512] / inv_count - mean * mean, FLOOR)
        om_ref[own_rows(part, z), :] = mean.astype(BF16)
        op_ref[own_rows(part, z), :] = (1.0 / var).astype(BF16)
        for cp in up_copies(part, z):
            cp.start()

    def o_view(ref, part):
        def view(r, s, n):
            start = pl.multiple_of(((r * 2 + part) * 16 + s) * ROWS, ROWS)
            return ref.at[pl.ds(start, n * ROWS)]
        return view

    of = [
        Flood([o_view(om_ref, t), o_view(op_ref, t)], o_s.at[t], o_r.at[t], slot[t], other[t], orders[t], core, c)
        for t in range(2)
    ]
    for part in range(2):
        for cp in up_copies(part, 1 - z):
            cp.wait_recv()
        of[part].start()

    def o_step(k):
        for t in range(2):
            of[t].arrive(k)

    both = [pl.ds(base[part], ROWS) for part in range(2)]
    mean_b = jnp.concatenate([om_ref[r, :] for r in both], axis=0)
    prec_b = jnp.concatenate([op_ref[r, :] for r in both], axis=0)
    mean_f, prec_f = mean_b.astype(F32), prec_b.astype(F32)
    prod_f = (mean_f * prec_f).astype(BF16).astype(F32)
    minus2 = (-2.0 * prod_f).astype(BF16)
    const = jnp.sum(mean_f * prod_f - jnp.log(prec_f), axis=1, keepdims=True)
    nt = (((1,), (1,)), ((), ()))

    def rescore(f, ch):
        @pl.loop(0, 4)
        def _(t):
            r = pl.ds(pl.multiple_of(t * 512, 512), 512)
            qt = lax.dot_general(prec_b, sq[f, ch, r, :], nt, preferred_element_type=F32)
            qt += lax.dot_general(minus2, xs[f, ch, r, :], nt, preferred_element_type=F32)
            v = jnp.sum((qt + const) * post[f, ch, :, r].astype(F32), axis=0, keepdims=True)
            for i in range(4):
                s = t * 4 + i
                qb[ch, s if f == 0 else rev4(s), f : f + 1, :] = v[:, i * 128 : (i + 1) * 128]

    rescore(0, 1 - c)
    rescore(1, 1 - c)

    def q_copy(i, src, dst, dev):
        return pltpu.make_async_remote_copy(
            src_ref=src, dst_ref=dst, send_sem=q_s.at[i], recv_sem=q_r.at[i],
            device_id={"states": dev}, device_id_type=MESH,
        )

    q_copies = [q_copy(0, qb.at[1 - c], rq, core)]
    q_copies[0].start()
    o_step(0)
    rescore(0, c)
    o_step(1)
    rescore(1, c)
    q_copies[0].wait_recv()
    summed = qb[c] + rq[...]
    qb[c] = summed
    bits = (v3, v2, v1, v0)
    dims = (3, 2, 1, 0)
    srcs = (qb.at[c], q8, q4, q2)
    sums = (q8, q4, q2, q1)
    recvs = (r8, r4, r2, r1)
    for i in range(4):
        n = 8 >> i
        b = bits[i]
        cp = q_copy(i + 1, srcs[i].at[pl.ds((1 - b) * n, n)], recvs[i], near[dims[i]])
        cp.start()
        q_copies.append(cp)
        if i == 1:
            o_step(2)
        cp.wait_recv()
        sums[i][...] = srcs[i][pl.ds(b * n, n)] + recvs[i][...]

    def h_copy(d):
        return pltpu.make_async_remote_copy(
            src_ref=q1, dst_ref=rh.at[d - 1], send_sem=h_s.at[d - 1], recv_sem=h_r.at[d - 1],
            device_id={"frames": (hi + d) % 4}, device_id_type=MESH,
        )

    for d in range(1, 4):
        h_copy(d).start()
    for d in range(1, 4):
        h_copy(d).wait_recv()
    quad = q1[0] + rh[0, 0] + rh[1, 0] + rh[2, 0]
    w_sum = jnp.sum(w_t, axis=0, keepdims=True)
    for f in range(2):
        score_ref[f : f + 1, :] = -0.5 * quad[f : f + 1, :] / (D * w_sum[:, f * 128 : (f + 1) * 128])

    o_step(3)
    for k in range(-1, 4):
        for t in range(2):
            of[t].arrive_core(k)

    gf.finish()
    for f in range(2):
        xf[f].finish()
        of[f].finish()
        acc_copy(f).wait_send()
        for cp in up_copies(f, z):
            cp.wait_send()
    for cp in q_copies:
        cp.wait_send()
    for d in range(1, 4):
        h_copy(d).wait_send()


def per_device(features, state_ids, weights):
    vm = pl.BlockSpec(memory_space=pltpu.VMEM)
    dma = pltpu.SemaphoreType.DMA
    states = 64 * ROWS
    means, precs, score = pl.pallas_call(
        kernel,
        out_shape=(
            jax.ShapeDtypeStruct((states, W), BF16),
            jax.ShapeDtypeStruct((states, W), BF16),
            jax.ShapeDtypeStruct((2, 128), F32),
        ),
        in_specs=[vm] * 3,
        out_specs=(vm,) * 3,
        scratch_shapes=[
            pltpu.VMEM((2, 2, 2048, W), BF16),
            pltpu.VMEM((2, 2, 2048, W), BF16),
            pltpu.VMEM((2, 16, 64, 256), I16),
            pltpu.VMEM((2, 2, 2 * ROWS, 2048), BF16),
            pltpu.VMEM((2 * ROWS, 640), F32),
            pltpu.VMEM((2, OWN, 640), F32),
            pltpu.VMEM((2, 16, 2, 128), F32),
            pltpu.VMEM((16, 2, 128), F32),
            *[pltpu.VMEM((n, 2, 128), F32) for n in (8, 4, 2, 1)],
            *[pltpu.VMEM((n, 2, 128), F32) for n in (8, 4, 2, 1)],
            pltpu.VMEM((3, 1, 2, 128), F32),
            dma((21, 1)), dma((21, 1)),
            dma((2, 21, 1)), dma((2, 21, 1)),
            dma((2, 21, 2)), dma((2, 21, 2)),
            dma((6,)), dma((6,)),
            dma((5,)), dma((5,)),
            dma((3,)), dma((3,)),
        ],
        compiler_params=pltpu.CompilerParams(
            collective_id=0, has_side_effects=True, vmem_limit_bytes=60 << 20
        ),
        name="fused",
    )(features, state_ids, weights)
    return means, precs, score.reshape(-1)


def solution(mesh):
    return jax.shard_map(
        per_device,
        mesh=mesh,
        in_specs=(P("states", "frames"), P("states", None), P("states", None)),
        out_specs=(P(None, "frames"), P(None, "frames"), P("states")),
        check_vma=False,
    )
```

```python
import jax
import jax.numpy as jnp
from jax import lax
from jax.experimental import pallas as pl
from jax.experimental.pallas import tpu as pltpu
from jax.sharding import PartitionSpec as P

MESH = pl.DeviceIdType.MESH
F32, BF16, I16, I32 = jnp.float32, jnp.bfloat16, jnp.int16, jnp.int32
D = 1024
W = 256
ROWS = 96
OWN = 48
FLOOR = 0.25
HOPS = ((0,), (1, 2, 4, 8), (3, 5, 6, 9, 10, 12), (7, 11, 13, 14), (15,))


def flip(s, mask):
    for k in range(4):
        if mask >> k & 1:
            s = s + 2**k * (1 - 2 * ((s // 2**k) % 2))
    return s


def rev4(s):
    return (s % 2) * 8 + ((s // 2) % 2) * 4 + ((s // 4) % 2) * 2 + s // 8


def gray(r):
    return (r + r // 2) % 2 + 2 * (r // 2)


class Flood:
    def __init__(self, views, ssem, rsem, slot, slot_other, partners, core, c):
        self.views, self.ssem, self.rsem = views, ssem, rsem
        self.slot, self.slot_other, self.partners, self.core, self.c = slot, slot_other, partners, core, c

    def _copies(self, region, s, i, device):
        return [
            pltpu.make_async_remote_copy(
                src_ref=view(region, s), dst_ref=view(region, s), send_sem=self.ssem.at[i, a],
                recv_sem=self.rsem.at[i, a], device_id={"states": device}, device_id_type=MESH,
            )
            for a, view in enumerate(self.views)
        ]

    def _out(self, m, k):
        return self._copies(self.c, flip(self.slot, m), m | 1 << k, self.partners[k])

    def _in(self, m):
        return self._copies(self.c, flip(self.slot, m), m, self.partners[m.bit_length() - 1])

    def _core_out(self, m):
        return self._copies(self.c, flip(self.slot, m), 16 + m, self.core)

    def _core_in(self, m):
        return self._copies(1 - self.c, flip(self.slot_other, m), 16 + m, self.core)

    def spread(self, m):
        for k in range(m.bit_length(), 4):
            for cp in self._out(m, k):
                cp.start()
        for cp in self._core_out(m):
            cp.start()

    def arrive(self, m):
        for cp in self._in(m):
            cp.wait_recv()
        self.spread(m)

    def arrive_core(self, m):
        for cp in self._core_in(m):
            cp.wait_recv()

    def finish(self):
        for m in range(16):
            for k in range(m.bit_length(), 4):
                for cp in self._out(m, k):
                    cp.wait_send()
            for cp in self._core_out(m):
                cp.wait_send()


def kernel(
    x_hbm, ids_hbm, w_hbm, om_ref, op_ref, score_ref,
    x_in, ids_in, w_in, xs, sq, g, post, acc, racc, occ, oc, roc, cnt, qb, rq, qy, ry, qx, rx, q1, rh,
    i_s, g_s, g_r, x_s, x_r, o_s, o_r, z_s, z_r, q_s, q_r, h_s, h_r,
):
    me = lax.axis_index("states")
    hi = lax.axis_index("frames")
    c = me % 2
    x = (me // 2) % 4
    y = (me // 8) % 4
    z = me // 32

    def device(z, y, x, c):
        return ((z * 4 + y) * 4 + x) * 2 + c

    p = x + c * (y - x)
    q = y + c * (x - y)

    def at(p2, q2):
        return device(z, q2 + c * (p2 - q2), p2 + c * (q2 - p2), c)

    v0, v1, v2, v3 = (p + p // 2) % 2, p // 2, (q + q // 2) % 2, q // 2
    near = [at(p + 1 - 2 * (p % 2), q), at(3 - p, q), at(p, q + 1 - 2 * (q % 2)), at(p, 3 - q)]
    core = device(z, y, x, 1 - c)
    up = device(1 - z, y, x, c)
    slot = (v0 + 2 * v1 + 4 * v2 + 8 * v3, v3 + 2 * v2 + 4 * v1 + 8 * v0)
    other = (v2 + 2 * v3 + 4 * v0 + 8 * v1, v1 + 2 * v0 + 4 * v3 + 8 * v2)

    barrier = pltpu.get_barrier_semaphore()
    for d in near + [at((p + 2) % 4, q), at(p, (q + 2) % 4), core, up]:
        pl.semaphore_signal(barrier, inc=1, device_id={"states": d}, device_id_type=MESH)
    for d in range(1, 4):
        pl.semaphore_signal(barrier, inc=1, device_id={"frames": (hi + d) % 4}, device_id_type=MESH)

    loads = [
        pltpu.make_async_copy(src, dst, i_s.at[i])
        for i, (src, dst) in enumerate(((ids_hbm, ids_in), (w_hbm, w_in), (x_hbm, x_in)))
    ]
    for cp in loads:
        cp.start()
    acc[...] = jnp.zeros_like(acc)
    occ[...] = jnp.zeros_like(occ)
    loads[0].wait()
    loads[1].wait()
    w_t = w_in[...].astype(BF16).astype(F32)
    g[c, slot[0], 0:32, :] = ids_in[...].astype(I16)
    g[c, slot[0], 32:64, :] = (w_t * 4096.0).astype(I32).astype(I16)
    loads[2].wait()
    for f in range(2):
        xs[f, c, pl.ds(pl.multiple_of(slot[f] * 128, 128), 128), :] = x_in[f * 128 : (f + 1) * 128, :]

    base = [pl.multiple_of(((c * 2 + part) * 16 + slot[part]) * ROWS, ROWS) for part in range(2)]
    iota = lax.broadcasted_iota(I32, (ROWS, 128), 0)
    rows = jnp.concatenate([(iota + base[0]).astype(I16), (iota + base[1]).astype(I16)], axis=0)

    def build(ch, s):
        ids = g[ch, s, 0:32, :].astype(I32)
        wv = g[ch, s, 32:64, :].astype(I32).astype(F32) * (1.0 / 4096.0)
        for f in range(2):
            lanes = slice(f * 128, (f + 1) * 128)
            block = jnp.zeros((2 * ROWS, 128), BF16)
            for j in range(32):
                idj = jnp.broadcast_to(ids[j : j + 1, lanes].astype(I16), (2 * ROWS, 128))
                wj = jnp.broadcast_to(wv[j : j + 1, lanes].astype(BF16), (2 * ROWS, 128))
                block = jnp.where(rows == idj, wj, block)
            col = pl.multiple_of((s if f == 0 else rev4(s)) * 128, 128)
            post[f, ch, :, pl.ds(col, 128)] = block
            occ[...] += block.astype(F32)

    def build_all(ch, first, h):
        def body(_, left):
            s = first
            for k in range(4):
                s = s + 2**k * ((left // 2**k) % 2) * (1 - 2 * ((first // 2**k) % 2))
            build(ch, s)
            return left // 16

        lax.fori_loop(0, len(HOPS[h]), body, jnp.int32(sum(m << 4 * i for i, m in enumerate(HOPS[h]))))

    def moments(f, ch, b):
        r = pl.ds(pl.multiple_of(b * 512, 512), 512)
        xv = xs[f, ch, r, :]
        xw = xv.astype(F32)
        sv = (xw * xw).astype(BF16)
        sq[f, ch, r, :] = sv
        pv = post[f, ch, :, r]
        acc[:, 0:256] += jnp.dot(pv, xv, preferred_element_type=F32)
        acc[:, 256:512] += jnp.dot(pv, sv, preferred_element_type=F32)

    def g_view(r, s):
        return g.at[r, s]

    def x_view(f):
        return lambda r, s: xs.at[f, r, pl.ds(pl.multiple_of(s * 128, 128), 128)]

    orders = (near, near[::-1])
    gf = Flood([g_view], g_s, g_r, slot[0], other[0], near, core, c)
    xf = [Flood([x_view(f)], x_s.at[f], x_r.at[f], slot[f], other[f], orders[f], core, c) for f in range(2)]

    def g_hop(h):
        for m in HOPS[h]:
            gf.arrive(m)

    def g_core(h):
        for m in HOPS[h]:
            gf.arrive_core(m)

    def x_hop(h):
        for m in HOPS[h]:
            for f in range(2):
                xf[f].arrive(m)

    def x_core(h):
        for m in HOPS[h]:
            for f in range(2):
                xf[f].arrive_core(m)

    with jax.named_scope("a0_barrier"):
        pl.semaphore_wait(barrier, 11)
    gf.spread(0)
    with jax.named_scope("b0_build"):
        build(c, slot[0])
    with jax.named_scope("b1_gcore0"):
        g_core(0)
        build(1 - c, other[0])
    with jax.named_scope("b2_ghop1"):
        g_hop(1)
    for f in range(2):
        xf[f].spread(0)
    with jax.named_scope("b3_build"):
        build_all(c, slot[0], 1)
    with jax.named_scope("b4_gcore1"):
        g_core(1)
    with jax.named_scope("b5_build"):
        build_all(1 - c, other[0], 1)
    with jax.named_scope("b6_ghop2"):
        g_hop(2)
    with jax.named_scope("b7_xhop1"):
        x_hop(1)
    with jax.named_scope("b8_build"):
        build_all(c, slot[0], 2)
    with jax.named_scope("c0_ghop3"):
        g_hop(3)
    with jax.named_scope("c1_gcore2"):
        g_core(2)
    with jax.named_scope("c2_build"):
        build_all(1 - c, other[0], 2)
    with jax.named_scope("c3_xhop2"):
        x_hop(2)
    with jax.named_scope("c4_ghop4"):
        g_hop(4)
    with jax.named_scope("c5_build"):
        build_all(c, slot[0], 3)
    with jax.named_scope("c6_gcore3"):
        g_core(3)
    with jax.named_scope("c7_build"):
        build_all(1 - c, other[0], 3)
    with jax.named_scope("c8_xhop3"):
        x_hop(3)
    with jax.named_scope("c9_build"):
        build(c, flip(slot[0], 15))
        g_core(4)
        build(1 - c, flip(other[0], 15))

    oc[...] = jnp.zeros_like(oc)
    oc[0:1, 0:192] = jnp.sum(jnp.transpose(occ[...]), axis=0, keepdims=True)

    def up_copy(i, src, dst):
        return pltpu.make_async_remote_copy(
            src_ref=src, dst_ref=dst, send_sem=z_s.at[i], recv_sem=z_r.at[i],
            device_id={"states": up}, device_id_type=MESH,
        )

    oc_copy = up_copy(6, oc, roc)
    oc_copy.start()

    def quarter(s, mask):
        return flip(s, mask) // 4

    with jax.named_scope("d0_xcore"):
        for h in range(3):
            x_core(h)
    with jax.named_scope("d1_mom"):
        for mask in (0, 4, 8):
            if mask == 4:
                x_core(3)
            for f in range(2):
                moments(f, c, quarter(slot[f], mask))
                moments(f, 1 - c, quarter(other[f], mask))
    with jax.named_scope("d2_xhop4"):
        x_hop(4)
    with jax.named_scope("d3_mom"):
        for f in range(2):
            moments(f, c, quarter(slot[f], 12))
    with jax.named_scope("d4_xcore4"):
        x_core(4)
    with jax.named_scope("d5_mom"):
        for f in range(2):
            moments(f, 1 - c, quarter(other[f], 12))

    def acc_copy(part):
        return up_copy(part, acc.at[pl.ds(pl.multiple_of(part * ROWS + (1 - z) * OWN, 8), OWN)], racc.at[part])

    def own_rows(part, zz):
        return pl.ds(pl.multiple_of(base[part] + zz * OWN, 16), OWN)

    def up_copies(part, zz):
        return [
            up_copy(2 + part * 2 + a, ref.at[own_rows(part, zz)], ref.at[own_rows(part, zz)])
            for a, ref in enumerate((om_ref, op_ref))
        ]

    for part in range(2):
        acc_copy(part).start()
    oc_copy.wait_recv()
    cnt[...] = jnp.transpose(jnp.broadcast_to(oc[0:1, :] + roc[0:1, :], (128, 256)))
    for part in range(2):
        with jax.named_scope("e0_accwait"):
            acc_copy(part).wait_recv()
        mine = pl.ds(pl.multiple_of(part * ROWS + z * OWN, 8), OWN)
        total = acc[mine, :] + racc[part]
        count = jnp.concatenate([cnt[mine, :], cnt[mine, :]], axis=1)
        mean = total[:, 0:256] / count
        var = jnp.maximum(total[:, 256:512] / count - mean * mean, FLOOR)
        om_ref[own_rows(part, z), :] = mean.astype(BF16)
        op_ref[own_rows(part, z), :] = (1.0 / var).astype(BF16)
        for cp in up_copies(part, z):
            cp.start()

    def o_view(ref, part):
        def view(r, s):
            return ref.at[pl.ds(pl.multiple_of(((r * 2 + part) * 16 + s) * ROWS, ROWS), ROWS)]
        return view

    of = [
        Flood([o_view(om_ref, t), o_view(op_ref, t)], o_s.at[t], o_r.at[t], slot[t], other[t], orders[t], core, c)
        for t in range(2)
    ]
    for part in range(2):
        with jax.named_scope("e1_upwait"):
            for cp in up_copies(part, 1 - z):
                cp.wait_recv()
        of[part].spread(0)

    def o_hop(h):
        for m in HOPS[h]:
            for t in range(2):
                of[t].arrive(m)

    both = [pl.ds(base[part], ROWS) for part in range(2)]
    mean_b = jnp.concatenate([om_ref[r, :] for r in both], axis=0)
    prec_b = jnp.concatenate([op_ref[r, :] for r in both], axis=0)
    mean_f, prec_f = mean_b.astype(F32), prec_b.astype(F32)
    prod_f = (mean_f * prec_f).astype(BF16).astype(F32)
    minus2 = (-2.0 * prod_f).astype(BF16)
    const = jnp.sum(mean_f * prod_f - jnp.log(prec_f), axis=1, keepdims=True)
    nt = (((1,), (1,)), ((), ()))

    def rescore(f, ch):
        @pl.loop(0, 4)
        def _(t):
            r = pl.ds(pl.multiple_of(t * 512, 512), 512)
            qt = lax.dot_general(prec_b, sq[f, ch, r, :], nt, preferred_element_type=F32)
            qt += lax.dot_general(minus2, xs[f, ch, r, :], nt, preferred_element_type=F32)
            v = jnp.sum((qt + const) * post[f, ch, :, r].astype(F32), axis=0, keepdims=True)
            for i in range(4):
                s = t * 4 + i
                qb[ch, s if f == 0 else rev4(s), f : f + 1, :] = v[:, i * 128 : (i + 1) * 128]

    def q_copy(i, src, dst, dev):
        return pltpu.make_async_remote_copy(
            src_ref=src, dst_ref=dst, send_sem=q_s.at[i], recv_sem=q_r.at[i],
            device_id={"states": dev}, device_id_type=MESH,
        )

    with jax.named_scope("f0_rescore"):
        rescore(0, 1 - c)
        rescore(1, 1 - c)
    q_core = q_copy(0, qb.at[1 - c], rq, core)
    q_core.start()
    with jax.named_scope("f1_rescore"):
        rescore(0, c)
        rescore(1, c)
    with jax.named_scope("f2_qcore"):
        q_core.wait_recv()
    qy[...] = qb[c] + rq[...]
    q_y = [q_copy(d, qy.at[pl.ds(gray((q + d) % 4) * 4, 4)], ry.at[d - 1], at(p, (q + d) % 4)) for d in range(1, 4)]
    for cp in q_y:
        cp.start()
    with jax.named_scope("f3_ohop1"):
        o_hop(1)
    with jax.named_scope("f4_qy"):
        for cp in q_y:
            cp.wait_recv()
    qx[...] = qy[pl.ds(gray(q) * 4, 4)] + ry[0] + ry[1] + ry[2]
    q_x = [q_copy(3 + d, qx.at[pl.ds(gray((p + d) % 4), 1)], rx.at[d - 1], at((p + d) % 4, q)) for d in range(1, 4)]
    for cp in q_x:
        cp.start()
    with jax.named_scope("f5_ohop2"):
        o_hop(2)
    with jax.named_scope("f6_qx"):
        for cp in q_x:
            cp.wait_recv()
    q1[...] = qx[pl.ds(gray(p), 1)] + rx[0] + rx[1] + rx[2]

    def h_copy(d):
        return pltpu.make_async_remote_copy(
            src_ref=q1, dst_ref=rh.at[d - 1], send_sem=h_s.at[d - 1], recv_sem=h_r.at[d - 1],
            device_id={"frames": (hi + d) % 4}, device_id_type=MESH,
        )

    for d in range(1, 4):
        h_copy(d).start()
    with jax.named_scope("g0_ohop3"):
        o_hop(3)
    with jax.named_scope("g1_h"):
        for d in range(1, 4):
            h_copy(d).wait_recv()
    quad = q1[0] + rh[0, 0] + rh[1, 0] + rh[2, 0]
    w_sum = jnp.sum(w_t, axis=0, keepdims=True)
    for f in range(2):
        score_ref[f : f + 1, :] = -0.5 * quad[f : f + 1, :] / (D * w_sum[:, f * 128 : (f + 1) * 128])
    with jax.named_scope("g2_ohop4"):
        o_hop(4)
    with jax.named_scope("g3_ocore"):
        for m in range(16):
            for t in range(2):
                of[t].arrive_core(m)

    with jax.named_scope("g4_finish"):
        gf.finish()
        oc_copy.wait_send()
        q_core.wait_send()
        for f in range(2):
            xf[f].finish()
            of[f].finish()
            acc_copy(f).wait_send()
            for cp in up_copies(f, z):
                cp.wait_send()
        for cp in q_y + q_x:
            cp.wait_send()
        for d in range(1, 4):
            h_copy(d).wait_send()


def per_device(features, state_ids, weights):
    hbm = pl.BlockSpec(memory_space=pl.ANY)
    vm = pl.BlockSpec(memory_space=pltpu.VMEM)
    dma = pltpu.SemaphoreType.DMA
    states = 64 * ROWS
    means, precs, score = pl.pallas_call(
        kernel,
        out_shape=(
            pltpu.VMEM((states, W), BF16),
            pltpu.VMEM((states, W), BF16),
            pltpu.VMEM((2, 128), F32),
        ),
        in_specs=[hbm] * 3,
        out_specs=(vm,) * 3,
        scratch_shapes=[
            pltpu.VMEM((256, W), BF16),
            pltpu.VMEM((32, 256), I32),
            pltpu.VMEM((32, 256), F32),
            pltpu.VMEM((2, 2, 2048, W), BF16),
            pltpu.VMEM((2, 2, 2048, W), BF16),
            pltpu.VMEM((2, 16, 64, 256), I16),
            pltpu.VMEM((2, 2, 2 * ROWS, 2048), BF16),
            pltpu.VMEM((2 * ROWS, 512), F32),
            pltpu.VMEM((2, OWN, 512), F32),
            pltpu.VMEM((2 * ROWS, 128), F32),
            pltpu.VMEM((8, 256), F32),
            pltpu.VMEM((8, 256), F32),
            pltpu.VMEM((256, 128), F32),
            pltpu.VMEM((2, 16, 2, 128), F32),
            pltpu.VMEM((16, 2, 128), F32),
            pltpu.VMEM((16, 2, 128), F32),
            pltpu.VMEM((3, 4, 2, 128), F32),
            pltpu.VMEM((4, 2, 128), F32),
            pltpu.VMEM((3, 1, 2, 128), F32),
            pltpu.VMEM((1, 2, 128), F32),
            pltpu.VMEM((3, 1, 2, 128), F32),
            dma((3,)),
            dma((32, 1)), dma((32, 1)),
            dma((2, 32, 1)), dma((2, 32, 1)),
            dma((2, 32, 2)), dma((2, 32, 2)),
            dma((7,)), dma((7,)),
            dma((7,)), dma((7,)),
            dma((3,)), dma((3,)),
        ],
        compiler_params=pltpu.CompilerParams(
            collective_id=0, has_side_effects=True, vmem_limit_bytes=40 << 20
        ),
        name="fused",
    )(features, state_ids.T, weights.T)
    return means, precs, score.reshape(-1)


def solution(mesh):
    return jax.shard_map(
        per_device,
        mesh=mesh,
        in_specs=(P("states", "frames"), P("states", None), P("states", None)),
        out_specs=(P(None, "frames"), P(None, "frames"), P("states")),
        check_vma=False,
    )
```

```python
import jax
import jax.numpy as jnp
from jax import lax
from jax.experimental import pallas as pl
from jax.experimental.pallas import tpu as pltpu
from jax.sharding import PartitionSpec as P

MESH = pl.DeviceIdType.MESH
F32, BF16, I16, I32 = jnp.float32, jnp.bfloat16, jnp.int16, jnp.int32
D = 1024
W = 256
ROWS = 96
OWN = 48
LATE = 32
FLOOR = 0.25
HOPS = ((0,), (1, 2, 4, 8), (3, 5, 6, 9, 10, 12), (7, 11, 13, 14), (15,))
GROUPS = ((1, 2), (4, 8), (3, 5, 6), (9, 10, 12), (7, 11, 13, 14), (15,))
LATER = ((1, 2, 4, 8), (3, 5, 6, 9, 10, 12), (7, 11, 13, 14, 15))


def flip(s, mask):
    for k in range(4):
        if mask >> k & 1:
            s = s + 2**k * (1 - 2 * ((s // 2**k) % 2))
    return s


def rev4(s):
    return (s % 2) * 8 + ((s // 2) % 2) * 4 + ((s // 4) % 2) * 2 + s // 8


def gray(r):
    return (r + r // 2) % 2 + 2 * (r // 2)


def place_of(groups, m):
    return [n for n, group in enumerate(groups) if m in group][0]


def landed(ref, sem):
    pltpu.make_async_copy(ref, ref, sem).wait()


def push(src, dst, send, recv, device):
    return pltpu.make_async_remote_copy(
        src_ref=src, dst_ref=dst, send_sem=send, recv_sem=recv, device_id=device, device_id_type=MESH
    )


class Flood:
    def __init__(self, view, slot, partners, core, c, send, recv, core_recv, first=None, up=None, up_view=None, up_recv=None):
        self.view, self.slot, self.partners, self.core, self.c = view, slot, partners, core, c
        self.send, self.recv, self.core_recv, self.first = send, recv, core_recv, first
        self.up, self.up_view, self.up_recv = up, up_view, up_recv

    def _pass(self, m, view, recv, device):
        dst = view(self.c, flip(self.slot, m))
        src = self.first if m == 0 and self.first is not None else dst
        push(src, dst, self.send, recv, {"states": device}).start()

    def start(self, ks):
        for k in ks:
            self._pass(0, self.view, self.recv(1 << k), self.partners[k])

    def start_core(self):
        self._pass(0, self.view, self.core_recv(0), self.core)

    def forward(self, m):
        for k in range(m.bit_length(), 4):
            self._pass(m, self.view, self.recv(m | 1 << k), self.partners[k])
        if self.up_view:
            self._pass(m, self.up_view, self.up_recv(m), self.up)
        self._pass(m, self.view, self.core_recv(m), self.core)


def kernel(
    x_hbm, ids_hbm, w_hbm, out, score_ref,
    x_in, ids_in, w_in, xs, g, post, acc, racc, occ, oc, roc, cnt, tb, qb, rq, qy, ry, qx, rx, q1, rh,
    i_s, g_s, g_r, g_c, x_s, x_r, x_c, o_s, o_r, t_r, u_r, o_c, acc_s, acc_r, tb_s, tb_r, oc_s, oc_r, l_s, q_s, q_r,
):
    me = lax.axis_index("states")
    hi = lax.axis_index("frames")
    c = me % 2
    x = (me // 2) % 4
    y = (me // 8) % 4
    z = me // 32

    def device(z, y, x, c):
        return ((z * 4 + y) * 4 + x) * 2 + c

    p = x + c * (y - x)
    q = y + c * (x - y)

    def at(p2, q2):
        return device(z, q2 + c * (p2 - q2), p2 + c * (q2 - p2), c)

    v0, v1, v2, v3 = (p + p // 2) % 2, p // 2, (q + q // 2) % 2, q // 2
    near = [at(p + 1 - 2 * (p % 2), q), at(3 - p, q), at(p, q + 1 - 2 * (q % 2)), at(p, 3 - q)]
    core = device(z, y, x, 1 - c)
    up = device(1 - z, y, x, c)
    slot = (v0 + 2 * v1 + 4 * v2 + 8 * v3, v3 + 2 * v2 + 4 * v1 + 8 * v0)
    other = (v2 + 2 * v3 + 4 * v0 + 8 * v1, v1 + 2 * v0 + 4 * v3 + 8 * v2)

    barrier = pltpu.get_barrier_semaphore()
    for d in near + [at((p + 2) % 4, q), at(p, (q + 2) % 4), core, up]:
        pl.semaphore_signal(barrier, inc=1, device_id={"states": d}, device_id_type=MESH)
    for d in range(1, 4):
        pl.semaphore_signal(barrier, inc=1, device_id={"frames": (hi + d) % 4}, device_id_type=MESH)

    loads = [
        pltpu.make_async_copy(src, dst, i_s.at[i])
        for i, (src, dst) in enumerate(((ids_hbm, ids_in), (w_hbm, w_in), (x_hbm, x_in)))
    ]
    for cp in loads:
        cp.start()
    acc[...] = jnp.zeros_like(acc)
    occ[...] = jnp.zeros_like(occ)
    loads[0].wait()
    loads[1].wait()
    w_t = w_in[...].astype(BF16).astype(F32)
    g[c * 16 + slot[0], 0:32, :] = ids_in[...].astype(I16)
    g[c * 16 + slot[0], 32:64, :] = (w_t * 4096.0).astype(I32).astype(I16)
    loads[2].wait()
    for f in range(2):
        xs[f, c, pl.ds(pl.multiple_of(slot[f] * 128, 128), 128), 0:W] = x_in[f * 128 : (f + 1) * 128, :]

    base = [pl.multiple_of(((c * 2 + part) * 16 + slot[part]) * ROWS, ROWS) for part in range(2)]
    iota = lax.broadcasted_iota(I32, (ROWS, 128), 0)
    rows = jnp.concatenate([(iota + base[0]).astype(I16), (iota + base[1]).astype(I16)], axis=0)

    def build(ch, s):
        ids = g[ch * 16 + s, 0:32, :].astype(I32)
        wv = g[ch * 16 + s, 32:64, :].astype(I32).astype(F32) * (1.0 / 4096.0)
        for f in range(2):
            lanes = slice(f * 128, (f + 1) * 128)
            block = jnp.zeros((2 * ROWS, 128), BF16)
            for j in range(32):
                idj = jnp.broadcast_to(ids[j : j + 1, lanes].astype(I16), (2 * ROWS, 128))
                wj = jnp.broadcast_to(wv[j : j + 1, lanes].astype(BF16), (2 * ROWS, 128))
                block = jnp.where(rows == idj, wj, block)
            col = pl.multiple_of((s if f == 0 else rev4(s)) * 128, 128)
            post[f, ch, :, pl.ds(col, 128)] = block
            occ[...] += block.astype(F32)

    def build_all(ch, first, h):
        def body(_, left):
            s = first
            for k in range(4):
                s = s + 2**k * ((left // 2**k) % 2) * (1 - 2 * ((first // 2**k) % 2))
            build(ch, s)
            return left // 16

        lax.fori_loop(0, len(HOPS[h]), body, jnp.int32(sum(m << 4 * i for i, m in enumerate(HOPS[h]))))

    def moments(f, ch, b):
        r = pl.ds(pl.multiple_of(b * 512, 512), 512)
        xw = xs[f, ch, r, 0:W].astype(F32)
        xs[f, ch, r, W : 2 * W] = (xw * xw).astype(BF16)
        acc[...] += jnp.dot(post[f, ch, :, r], xs[f, ch, r, :], preferred_element_type=F32)

    orders = (near, near[::-1])
    gf = Flood(
        lambda r, s: g.at[r * 16 + s], slot[0], near, core, c, g_s.at[0],
        lambda m: g_r.at[place_of(HOPS, m) - 1], lambda m: g_c.at[place_of(HOPS, m)],
    )
    xf = [
        Flood(
            lambda r, s, f=f: xs.at[f, r, pl.ds(pl.multiple_of(s * 128, 128), 128), 0:W], slot[f], orders[f], core, c,
            x_s.at[0], lambda m: x_r.at[place_of(GROUPS, m)], lambda m: x_c.at[max(m.bit_count(), 2) - 2],
        )
        for f in range(2)
    ]

    def g_hop(h):
        landed(g.at[0 : len(HOPS[h])], g_r.at[h - 1])
        for m in HOPS[h]:
            gf.forward(m)

    def g_core(h):
        landed(g.at[0 : len(HOPS[h])], g_c.at[h])

    def x_group(i):
        landed(xs.at[0, 0, 0 : len(GROUPS[i]) * 256, 0:W], x_r.at[i])
        for m in GROUPS[i]:
            for f in range(2):
                xf[f].forward(m)

    def x_core(i):
        landed(xs.at[:, 0, 0 : (11, 4, 1)[i] * 128, 0:W], x_c.at[i])

    def quarter(s, mask):
        return flip(s, mask) // 4

    def own_moments(mask):
        for f in range(2):
            moments(f, c, quarter(slot[f], mask))

    def core_moments(mask):
        for f in range(2):
            moments(f, 1 - c, quarter(other[f], mask))

    with jax.named_scope("a0_barrier"):
        pl.semaphore_wait(barrier, 11)
    gf.start(range(4))
    gf.start_core()
    for ks in ((0, 1), (2, 3)):
        for f in range(2):
            xf[f].start(ks)
    for f in range(2):
        xf[f].start_core()
    with jax.named_scope("b0_build"):
        build(c, slot[0])
    with jax.named_scope("b1_gcore0"):
        g_core(0)
        build(1 - c, other[0])
    with jax.named_scope("b2_ghop1"):
        g_hop(1)
    with jax.named_scope("b3_x12"):
        x_group(0)
    with jax.named_scope("b4_build"):
        build_all(c, slot[0], 1)
    with jax.named_scope("b5_x48"):
        x_group(1)
    with jax.named_scope("b6_gcore1"):
        g_core(1)
        build_all(1 - c, other[0], 1)
    with jax.named_scope("b7_ghop2"):
        g_hop(2)
    with jax.named_scope("b8_build"):
        build_all(c, slot[0], 2)
    with jax.named_scope("c0_x356"):
        x_group(2)
    with jax.named_scope("c1_ghop3"):
        g_hop(3)
    with jax.named_scope("c2_build"):
        g_core(2)
        build_all(1 - c, other[0], 2)
    with jax.named_scope("c3_x9"):
        x_group(3)
    with jax.named_scope("c4_build"):
        build_all(c, slot[0], 3)
    with jax.named_scope("c5_ghop4"):
        g_hop(4)
    with jax.named_scope("c6_build"):
        g_core(3)
        build_all(1 - c, other[0], 3)
    with jax.named_scope("c7_x7"):
        x_group(4)
    with jax.named_scope("c8_build"):
        build(c, flip(slot[0], 15))
        g_core(4)
        build(1 - c, flip(other[0], 15))

    oc[...] = jnp.zeros_like(oc)
    oc[0:1, 0:192] = jnp.sum(jnp.transpose(occ[...]), axis=0, keepdims=True)

    def up_push(src, dst, send, recv):
        return push(src, dst, send, recv, {"states": up})

    up_push(oc, roc, oc_s.at[0], oc_r.at[0]).start()

    with jax.named_scope("d0_mom"):
        own_moments(0)
        x_core(0)
        core_moments(0)
        own_moments(4)
        own_moments(8)
    with jax.named_scope("d1_x15"):
        x_group(5)
    with jax.named_scope("d2_mom"):
        x_core(1)
        core_moments(4)
        core_moments(8)
        own_moments(12)
    with jax.named_scope("d3_xcore4"):
        x_core(2)
    with jax.named_scope("d4_mom"):
        core_moments(12)

    for part in range(2):
        r = pl.ds(pl.multiple_of(part * ROWS + (1 - z) * OWN, 8), OWN)
        up_push(acc.at[r], racc.at[part], acc_s.at[0], acc_r.at[part]).start()

    def rows_of(part, r, s, first, n):
        return out.at[:, pl.ds(pl.multiple_of(((r * 2 + part) * 16 + s) * ROWS + first, 16), n)]

    def tb_rows(part, first, n):
        return tb.at[part, :, pl.ds(pl.multiple_of(first, 16), n)]

    mine, theirs = z * OWN, (1 - z) * OWN
    of, tf = [], []
    for t in range(2):
        of.append(
            Flood(
                lambda r, s, t=t: rows_of(t, r, s, mine, OWN), slot[t], orders[t], core, c, o_s.at[0],
                lambda m, t=t: o_r.at[t, place_of(GROUPS, m)], lambda m: o_c.at[0], tb_rows(t, mine, OWN),
                up, lambda r, s, t=t: rows_of(t, r, s, mine + LATE, OWN - LATE), lambda m: u_r.at[place_of(LATER, m)],
            )
        )
        tf.append(
            Flood(
                lambda r, s, t=t: rows_of(t, r, s, theirs, LATE), slot[t], orders[t], core, c, o_s.at[0],
                lambda m, t=t: t_r.at[t, place_of(GROUPS, m)], lambda m: o_c.at[0], tb_rows(t, theirs, LATE),
            )
        )

    def o_group(t, i):
        landed(out.at[:, 0 : len(GROUPS[i]) * OWN], o_r.at[t, i])
        for m in GROUPS[i]:
            of[t].forward(m)

    def t_group(t, i):
        landed(out.at[:, 0 : len(GROUPS[i]) * LATE], t_r.at[t, i])
        for m in GROUPS[i]:
            tf[t].forward(m)

    def late_rows(t, m):
        return rows_of(t, c, flip(slot[t], m), theirs + LATE, OWN - LATE)

    def u_group(i):
        landed(out.at[:, 0 : len(LATER[i]) * 2 * (OWN - LATE)], u_r.at[i])
        for m in LATER[i]:
            for t in range(2):
                push(late_rows(t, m), late_rows(t, m), o_s.at[0], o_c.at[0], {"states": core}).start()

    landed(roc, oc_r.at[0])
    cnt[...] = jnp.transpose(jnp.broadcast_to(oc[0:1, :] + roc[0:1, :], (128, 256)))
    for part in range(2):
        with jax.named_scope("e0_accwait"):
            landed(racc.at[part], acc_r.at[part])
        r = pl.ds(pl.multiple_of(part * ROWS + z * OWN, 8), OWN)
        total = acc[r, :] + racc[part]
        count = jnp.concatenate([cnt[r, :], cnt[r, :]], axis=1)
        mean = total[:, 0:W] / count
        var = jnp.maximum(total[:, W : 2 * W] / count - mean * mean, FLOOR)
        own = pl.ds(pl.multiple_of(mine, 16), OWN)
        tb[part, 0, own, :] = mean.astype(BF16)
        tb[part, 1, own, :] = (1.0 / var).astype(BF16)
        up_push(tb_rows(part, mine, OWN), tb_rows(part, mine, OWN), tb_s.at[0], tb_r.at[part]).start()
        of[part].start(range(4))
        of[part].start_core()
    for part in range(2):
        with jax.named_scope("e1_upwait"):
            landed(tb_rows(part, theirs, OWN), tb_r.at[part])
        tf[part].start(range(4))
        tf[part].start_core()
        push(tb_rows(part, theirs + LATE, OWN - LATE), late_rows(part, 0), o_s.at[0], o_c.at[0], {"states": core}).start()
        pltpu.make_async_copy(tb.at[part], rows_of(part, c, slot[part], 0, ROWS), l_s.at[0]).start()
        with jax.named_scope("e2_o12"):
            o_group(part, 0)

    mean_b = jnp.concatenate([tb[t, 0] for t in range(2)], axis=0)
    prec_b = jnp.concatenate([tb[t, 1] for t in range(2)], axis=0)
    mean_f, prec_f = mean_b.astype(F32), prec_b.astype(F32)
    prod_f = (mean_f * prec_f).astype(BF16).astype(F32)
    coeff = jnp.concatenate([(-2.0 * prod_f).astype(BF16), prec_b], axis=1)
    const = jnp.sum(mean_f * prod_f - jnp.log(prec_f), axis=1, keepdims=True)
    nt = (((1,), (1,)), ((), ()))

    def rescore(f, ch):
        @pl.loop(0, 4)
        def _(t):
            r = pl.ds(pl.multiple_of(t * 512, 512), 512)
            qt = lax.dot_general(coeff, xs[f, ch, r, :], nt, preferred_element_type=F32)
            v = jnp.sum((qt + const) * post[f, ch, :, r].astype(F32), axis=0, keepdims=True)
            for i in range(4):
                s = t * 4 + i
                qb[ch, s if f == 0 else rev4(s), f : f + 1, :] = v[:, i * 128 : (i + 1) * 128]

    def q_push(i, src, dst, dev):
        push(src, dst, q_s.at[i], q_r.at[i], dev).start()

    with jax.named_scope("f0_rescore"):
        rescore(0, 1 - c)
    with jax.named_scope("f1_o48"):
        for t in range(2):
            o_group(t, 1)
            t_group(t, 0)
    with jax.named_scope("f2_rescore"):
        rescore(1, 1 - c)
    q_push(0, qb.at[1 - c], rq, {"states": core})
    with jax.named_scope("f3_t48"):
        for t in range(2):
            t_group(t, 1)
            o_group(t, 2)
    with jax.named_scope("f4_rescore"):
        rescore(0, c)
    with jax.named_scope("f5_o9"):
        for t in range(2):
            o_group(t, 3)
    with jax.named_scope("f6_rescore"):
        rescore(1, c)
    with jax.named_scope("f7_qcore"):
        landed(rq, q_r.at[0])
    qy[...] = qb[c] + rq[...]
    for d in range(1, 4):
        q2 = (q + d) % 4
        q_push(1, qy.at[pl.ds(gray(q2) * 4, 4)], ry.at[d - 1], {"states": at(p, q2)})
    with jax.named_scope("g0_t3"):
        for t in range(2):
            t_group(t, 2)
            t_group(t, 3)
        u_group(0)
    with jax.named_scope("g1_qy"):
        landed(ry, q_r.at[1])
    qx[...] = qy[pl.ds(gray(q) * 4, 4)] + ry[0] + ry[1] + ry[2]
    for d in range(1, 4):
        p2 = (p + d) % 4
        q_push(2, qx.at[pl.ds(gray(p2), 1)], rx.at[d - 1], {"states": at(p2, q)})
    with jax.named_scope("g2_o7"):
        for t in range(2):
            o_group(t, 4)
        u_group(1)
    with jax.named_scope("g3_t7"):
        for t in range(2):
            t_group(t, 4)
    with jax.named_scope("g4_qx"):
        landed(rx, q_r.at[2])
    q1[...] = qx[pl.ds(gray(p), 1)] + rx[0] + rx[1] + rx[2]
    for d in range(1, 4):
        q_push(3, q1, rh.at[d - 1], {"frames": (hi + d) % 4})
    with jax.named_scope("g5_15"):
        for t in range(2):
            o_group(t, 5)
            t_group(t, 5)
    with jax.named_scope("g6_u"):
        u_group(2)
    with jax.named_scope("h0_h"):
        landed(rh, q_r.at[3])
    quad = q1[0] + rh[0, 0] + rh[1, 0] + rh[2, 0]
    w_sum = jnp.sum(w_t, axis=0, keepdims=True)
    for f in range(2):
        score_ref[f : f + 1, :] = -0.5 * quad[f : f + 1, :] / (D * w_sum[:, f * 128 : (f + 1) * 128])
    with jax.named_scope("h1_core"):
        landed(out.at[:, 0 : 32 * ROWS], o_c.at[0])
        landed(tb, l_s.at[0])

    with jax.named_scope("h2_finish"):
        landed(g.at[0:31], g_s.at[0])
        landed(xs.at[:, :, 0:1984, 0:W], x_s.at[0])
        landed(out.at[:, 0 : 2 * (31 * OWN + 31 * LATE + 31 * (OWN - LATE))], o_s.at[0])
        landed(oc, oc_s.at[0])
        landed(racc, acc_s.at[0])
        landed(tb.at[:, :, 0:OWN], tb_s.at[0])
        landed(rq, q_s.at[0])
        landed(ry, q_s.at[1])
        landed(rx, q_s.at[2])
        landed(rh, q_s.at[3])


def per_device(features, state_ids, weights):
    hbm = pl.BlockSpec(memory_space=pltpu.HBM)
    place = pl.BlockSpec(memory_space=pl.ANY)
    vm = pl.BlockSpec(memory_space=pltpu.VMEM)
    dma = pltpu.SemaphoreType.DMA
    states = 64 * ROWS
    both, score = pl.pallas_call(
        kernel,
        out_shape=(
            pltpu.VMEM((2, states, W), BF16),
            pltpu.VMEM((2, 128), F32),
        ),
        in_specs=[hbm] * 3,
        out_specs=(place, vm),
        scratch_shapes=[
            pltpu.VMEM((256, W), BF16),
            pltpu.VMEM((32, 256), I32),
            pltpu.VMEM((32, 256), F32),
            pltpu.VMEM((2, 2, 2048, 2 * W), BF16),
            pltpu.VMEM((32, 64, 256), I16),
            pltpu.VMEM((2, 2, 2 * ROWS, 2048), BF16),
            pltpu.VMEM((2 * ROWS, 512), F32),
            pltpu.VMEM((2, OWN, 512), F32),
            pltpu.VMEM((2 * ROWS, 128), F32),
            pltpu.VMEM((8, 256), F32),
            pltpu.VMEM((8, 256), F32),
            pltpu.VMEM((256, 128), F32),
            pltpu.VMEM((2, 2, ROWS, W), BF16),
            pltpu.VMEM((2, 16, 2, 128), F32),
            pltpu.VMEM((16, 2, 128), F32),
            pltpu.VMEM((16, 2, 128), F32),
            pltpu.VMEM((3, 4, 2, 128), F32),
            pltpu.VMEM((4, 2, 128), F32),
            pltpu.VMEM((3, 1, 2, 128), F32),
            pltpu.VMEM((1, 2, 128), F32),
            pltpu.VMEM((3, 1, 2, 128), F32),
            dma((3,)),
            dma((1,)), dma((4,)), dma((5,)),
            dma((1,)), dma((6,)), dma((3,)),
            dma((1,)), dma((2, 6)), dma((2, 6)), dma((3,)), dma((1,)),
            dma((1,)), dma((2,)),
            dma((1,)), dma((2,)),
            dma((1,)), dma((1,)),
            dma((1,)),
            dma((4,)), dma((4,)),
        ],
        compiler_params=pltpu.CompilerParams(
            collective_id=0, has_side_effects=True, vmem_limit_bytes=40 << 20
        ),
        name="fused",
    )(*[pltpu.with_memory_space_constraint(a, pltpu.HBM) for a in (features, state_ids.T, weights.T)])
    return both[0], both[1], score.reshape(-1)


def solution(mesh):
    return jax.shard_map(
        per_device,
        mesh=mesh,
        in_specs=(P("states", "frames"), P("states", None), P("states", None)),
        out_specs=(P(None, "frames"), P(None, "frames"), P("states")),
        check_vma=False,
    )
```

```python
import jax
import jax.numpy as jnp
from jax import lax
from jax.experimental import pallas as pl
from jax.experimental.pallas import tpu as pltpu
from jax.sharding import PartitionSpec as P

MESH = pl.DeviceIdType.MESH
F32, BF16, I16, I32 = jnp.float32, jnp.bfloat16, jnp.int16, jnp.int32
D = 1024
W = 256
ROWS = 96
OWN = 48
LATE = 32
FLOOR = 0.25
HOPS = ((0,), (1, 2, 4, 8), (3, 5, 6, 9, 10, 12), (7, 11, 13, 14), (15,))
GROUPS = ((1, 2), (4, 8), (3, 5, 6), (9, 10, 12), (7, 11, 13, 14), (15,))
LATER = ((1, 2, 4, 8), (3, 5, 6, 9, 10, 12), (7, 11, 13, 14, 15))

H = W // 2
ORDER = (
    "G0", "Xs0a", "Xs0b", "Xs1a", "G1", "GC1", "x0g1", "x0g0", "XCs0", "bo10", "bo11", "bc11", "G2", "bo20", "Xs1b",
    "x0g2", "bo21", "x1g0", "GC2", "bc21", "G3", "bo31", "bo30", "bc10", "x1g1", "GC3", "x0g3", "bo0", "mo0e0",
    "bc30", "GC0", "x0g4", "bc20", "XC00", "x1g2", "mo4e0", "bc0", "mo0e1", "G4", "bc31", "mo8e0", "bo4", "XC01",
    "GC4", "x0g5", "bc4", "x1g3", "XCs1", "mo12e0", "mc0e0", "occ", "mc8e0", "mc4e0", "XC02", "mc12e0", "A0", "x1g4",
    "x1g5", "XC11", "XC10", "mo8e1", "mo4e1", "mo12e1", "mc0e1", "mc8e1", "mc4e1", "XC12", "mc12e1", "A1", "AW0",
    "o0g0", "AW1", "TW0", "R03", "o0g1", "R01", "R04", "o0g2", "R02", "TW1", "o1g0", "R14", "R00", "R10", "o1g1",
    "R05", "o0g3", "t0g0", "t0g1", "R12", "R13", "R11", "U00", "t1g0", "Q0", "R15", "o1g2", "R07", "R06", "t1g1",
    "o0g4", "R17", "o1g3", "t0g3", "R16", "U10", "Q1", "t0g2", "t1g2", "o1g4", "o0g5", "Q2", "t0g4", "t1g3", "U01",
    "U11", "t1g4", "o1g5", "Q3", "U02", "t1g5", "t0g5", "U12", "Q4", "OC",
)


def flip(s, mask):
    for k in range(4):
        if mask >> k & 1:
            s = s + 2**k * (1 - 2 * ((s // 2**k) % 2))
    return s


def rev4(s):
    return (s % 2) * 8 + ((s // 2) % 2) * 4 + ((s // 4) % 2) * 2 + s // 8


def gray(r):
    return (r + r // 2) % 2 + 2 * (r // 2)


def place_of(groups, m):
    return [n for n, group in enumerate(groups) if m in group][0]


def landed(ref, sem):
    pltpu.make_async_copy(ref, ref, sem).wait()


def push(src, dst, send, recv, device):
    return pltpu.make_async_remote_copy(
        src_ref=src, dst_ref=dst, send_sem=send, recv_sem=recv, device_id=device, device_id_type=MESH
    )


class Flood:
    def __init__(self, view, slot, partners, core, c, send, recv, core_recv, first=None, up=None, up_view=None, up_recv=None):
        self.view, self.slot, self.partners, self.core, self.c = view, slot, partners, core, c
        self.send, self.recv, self.core_recv, self.first = send, recv, core_recv, first
        self.up, self.up_view, self.up_recv = up, up_view, up_recv

    def _pass(self, m, view, recv, device):
        dst = view(self.c, flip(self.slot, m))
        src = self.first if m == 0 and self.first is not None else dst
        push(src, dst, self.send, recv, {"states": device}).start()

    def start(self, ks):
        for k in ks:
            self._pass(0, self.view, self.recv(1 << k), self.partners[k])

    def start_core(self):
        self._pass(0, self.view, self.core_recv(0), self.core)

    def forward(self, m):
        for k in range(m.bit_length(), 4):
            self._pass(m, self.view, self.recv(m | 1 << k), self.partners[k])
        if self.up_view:
            self._pass(m, self.up_view, self.up_recv(m), self.up)
        self._pass(m, self.view, self.core_recv(m), self.core)


def kernel(
    x_hbm, ids_hbm, w_hbm, out, score_ref,
    x_in, ids_in, w_in, xs, g, post, acc, racc, occ, oc, roc, cnt, tb, co, cs, qb, rq, qy, ry, qx, rx, q1, rh,
    i_s, g_s, g_r, g_c, x_s, x_r, x_c, o_s, o_r, t_r, u_r, o_c, acc_s, acc_r, tb_s, tb_r, oc_s, oc_r, l_s, q_s, q_r,
):
    me = lax.axis_index("states")
    hi = lax.axis_index("frames")
    c = me % 2
    x = (me // 2) % 4
    y = (me // 8) % 4
    z = me // 32

    def device(z, y, x, c):
        return ((z * 4 + y) * 4 + x) * 2 + c

    p = x + c * (y - x)
    q = y + c * (x - y)

    def at(p2, q2):
        return device(z, q2 + c * (p2 - q2), p2 + c * (q2 - p2), c)

    v0, v1, v2, v3 = (p + p // 2) % 2, p // 2, (q + q // 2) % 2, q // 2
    near = [at(p + 1 - 2 * (p % 2), q), at(3 - p, q), at(p, q + 1 - 2 * (q % 2)), at(p, 3 - q)]
    core = device(z, y, x, 1 - c)
    up = device(1 - z, y, x, c)
    slot = (v0 + 2 * v1 + 4 * v2 + 8 * v3, v3 + 2 * v2 + 4 * v1 + 8 * v0)
    other = (v2 + 2 * v3 + 4 * v0 + 8 * v1, v1 + 2 * v0 + 4 * v3 + 8 * v2)

    barrier = pltpu.get_barrier_semaphore()
    for d in near + [at((p + 2) % 4, q), at(p, (q + 2) % 4), core, up]:
        pl.semaphore_signal(barrier, inc=1, device_id={"states": d}, device_id_type=MESH)
    for d in range(1, 4):
        pl.semaphore_signal(barrier, inc=1, device_id={"frames": (hi + d) % 4}, device_id_type=MESH)

    loads = [
        pltpu.make_async_copy(src, dst, i_s.at[i])
        for i, (src, dst) in enumerate(((ids_hbm, ids_in), (w_hbm, w_in), (x_hbm, x_in)))
    ]
    for cp in loads:
        cp.start()
    acc[...] = jnp.zeros_like(acc)
    occ[...] = jnp.zeros_like(occ)
    loads[0].wait()
    loads[1].wait()
    w_t = w_in[...].astype(BF16).astype(F32)
    g[c * 16 + slot[0], 0:32, :] = ids_in[...].astype(I16)
    g[c * 16 + slot[0], 32:64, :] = (w_t * 4096.0).astype(I32).astype(I16)
    loads[2].wait()
    for f in range(2):
        r = pl.ds(pl.multiple_of(slot[f] * 128, 128), 128)
        for e in range(2):
            xs[f, c, r, e * W : e * W + H] = x_in[f * 128 : (f + 1) * 128, e * H : (e + 1) * H]

    base = [pl.multiple_of(((c * 2 + part) * 16 + slot[part]) * ROWS, ROWS) for part in range(2)]
    iota = lax.broadcasted_iota(I32, (ROWS, 128), 0)
    rows = jnp.concatenate([(iota + base[0]).astype(I16), (iota + base[1]).astype(I16)], axis=0)

    def build(ch, s):
        ids = g[ch * 16 + s, 0:32, :].astype(I32)
        wv = g[ch * 16 + s, 32:64, :].astype(I32).astype(F32) * (1.0 / 4096.0)
        for f in range(2):
            lanes = slice(f * 128, (f + 1) * 128)
            block = jnp.zeros((2 * ROWS, 128), BF16)
            for j in range(32):
                idj = jnp.broadcast_to(ids[j : j + 1, lanes].astype(I16), (2 * ROWS, 128))
                wj = jnp.broadcast_to(wv[j : j + 1, lanes].astype(BF16), (2 * ROWS, 128))
                block = jnp.where(rows == idj, wj, block)
            col = pl.multiple_of((s if f == 0 else rev4(s)) * 128, 128)
            post[f, ch, :, pl.ds(col, 128)] = block
            occ[...] += block.astype(F32)

    def build_all(ch, first, masks):
        if len(masks) == 1:
            return build(ch, flip(first, masks[0]))

        def body(_, left):
            s = first
            for k in range(4):
                s = s + 2**k * ((left // 2**k) % 2) * (1 - 2 * ((first // 2**k) % 2))
            build(ch, s)
            return left // 16

        lax.fori_loop(0, len(masks), body, jnp.int32(sum(m << 4 * i for i, m in enumerate(masks))))

    def moments(f, ch, b, e):
        r = pl.ds(pl.multiple_of(b * 512, 512), 512)
        xw = xs[f, ch, r, e * W : e * W + H].astype(F32)
        xs[f, ch, r, e * W + H : (e + 1) * W] = (xw * xw).astype(BF16)
        acc[e] += jnp.dot(post[f, ch, :, r], xs[f, ch, r, e * W : (e + 1) * W], preferred_element_type=F32)

    orders = (near, near[::-1])
    gf = Flood(
        lambda r, s: g.at[r * 16 + s], slot[0], near, core, c, g_s.at[0],
        lambda m: g_r.at[place_of(HOPS, m) - 1], lambda m: g_c.at[place_of(HOPS, m)],
    )
    xf = [
        [
            Flood(
                lambda r, s, f=f, e=e: xs.at[f, r, pl.ds(pl.multiple_of(s * 128, 128), 128), e * W : e * W + H],
                slot[f], orders[f], core, c, x_s.at[0],
                lambda m, e=e: x_r.at[e, place_of(GROUPS, m)], lambda m, e=e: x_c.at[e, max(m.bit_count(), 2) - 2],
            )
            for f in range(2)
        ]
        for e in range(2)
    ]

    def g_hop(h):
        landed(g.at[0 : len(HOPS[h])], g_r.at[h - 1])
        for m in HOPS[h]:
            gf.forward(m)

    def g_core(h):
        landed(g.at[0 : len(HOPS[h])], g_c.at[h])

    def x_start(e, ks):
        for f in range(2):
            xf[e][f].start(ks)

    def x_start_core(e):
        for f in range(2):
            xf[e][f].start_core()

    def x_group(e, i):
        landed(xs.at[0, 0, 0 : len(GROUPS[i]) * 256, 0:H], x_r.at[e, i])
        for m in GROUPS[i]:
            for f in range(2):
                xf[e][f].forward(m)

    def x_core(e, i):
        landed(xs.at[:, 0, 0 : (11, 4, 1)[i] * 128, 0:H], x_c.at[e, i])

    def own_moments(mask, e):
        for f in range(2):
            moments(f, c, flip(slot[f], mask) // 4, e)

    def core_moments(mask, e):
        for f in range(2):
            moments(f, 1 - c, flip(other[f], mask) // 4, e)

    def up_push(src, dst, send, recv):
        push(src, dst, send, recv, {"states": up}).start()

    def occupancy():
        oc[...] = jnp.zeros_like(oc)
        oc[0:1, 0:192] = jnp.sum(jnp.transpose(occ[...]), axis=0, keepdims=True)
        up_push(oc, roc, oc_s.at[0], oc_r.at[0])

    def acc_send(e):
        for part in range(2):
            r = pl.ds(pl.multiple_of(part * ROWS + (1 - z) * OWN, 8), OWN)
            up_push(acc.at[e, r], racc.at[e, part], acc_s.at[0], acc_r.at[e])

    def rows_of(part, r, s, first, n, e):
        start = pl.multiple_of(((r * 2 + part) * 16 + s) * ROWS + first, 16)
        return out.at[:, pl.ds(start, n), e * H : (e + 1) * H]

    def tb_rows(part, first, n, e):
        return tb.at[part, :, pl.ds(pl.multiple_of(first, 16), n), e * H : (e + 1) * H]

    mine, theirs = z * OWN, (1 - z) * OWN
    of, tf = [[], []], [[], []]
    for e in range(2):
        for t in range(2):
            of[e].append(
                Flood(
                    lambda r, s, t=t, e=e: rows_of(t, r, s, mine, OWN, e), slot[t], orders[t], core, c, o_s.at[0],
                    lambda m, e=e: o_r.at[e, place_of(GROUPS, m)], lambda m: o_c.at[0], tb_rows(t, mine, OWN, e),
                    up, lambda r, s, t=t, e=e: rows_of(t, r, s, mine + LATE, OWN - LATE, e),
                    lambda m, e=e: u_r.at[e, place_of(LATER, m)],
                )
            )
            tf[e].append(
                Flood(
                    lambda r, s, t=t, e=e: rows_of(t, r, s, theirs, LATE, e), slot[t], orders[t], core, c, o_s.at[0],
                    lambda m, e=e: t_r.at[e, place_of(GROUPS, m)], lambda m: o_c.at[0], tb_rows(t, theirs, LATE, e),
                )
            )

    def o_group(e, i):
        landed(out.at[:, 0 : len(GROUPS[i]) * 2 * OWN, 0:H], o_r.at[e, i])
        for m in GROUPS[i]:
            for t in range(2):
                of[e][t].forward(m)

    def t_group(e, i):
        landed(out.at[:, 0 : len(GROUPS[i]) * 2 * LATE, 0:H], t_r.at[e, i])
        for m in GROUPS[i]:
            for t in range(2):
                tf[e][t].forward(m)

    def late_rows(t, m, e):
        return rows_of(t, c, flip(slot[t], m), theirs + LATE, OWN - LATE, e)

    def u_group(e, i):
        landed(out.at[:, 0 : len(LATER[i]) * 2 * (OWN - LATE), 0:H], u_r.at[e, i])
        for m in LATER[i]:
            for t in range(2):
                push(late_rows(t, m, e), late_rows(t, m, e), o_s.at[0], o_c.at[0], {"states": core}).start()

    def update(e):
        landed(racc.at[e], acc_r.at[e])
        if e == 0:
            landed(roc, oc_r.at[0])
            cnt[...] = jnp.transpose(jnp.broadcast_to(oc[0:1, :] + roc[0:1, :], (128, 256)))
        own = pl.ds(pl.multiple_of(mine, 16), OWN)
        for part in range(2):
            r = pl.ds(pl.multiple_of(part * ROWS + z * OWN, 8), OWN)
            total = acc[e, r, :] + racc[e, part]
            count = cnt[r, :]
            mean = total[:, 0:H] / count
            var = jnp.maximum(total[:, H:W] / count - mean * mean, FLOOR)
            tb[part, 0, own, e * H : (e + 1) * H] = mean.astype(BF16)
            tb[part, 1, own, e * H : (e + 1) * H] = (1.0 / var).astype(BF16)
        for part in range(2):
            up_push(tb_rows(part, mine, OWN, e), tb_rows(part, mine, OWN, e), tb_s.at[0], tb_r.at[e])
        for ks in ((0, 1), (2, 3)):
            for part in range(2):
                of[e][part].start(ks)
        for part in range(2):
            of[e][part].start_core()

    def table(e):
        landed(tb.at[:, :, 0:OWN, 0:H], tb_r.at[e])
        for ks in ((0, 1), (2, 3)):
            for part in range(2):
                tf[e][part].start(ks)
        for part in range(2):
            tf[e][part].start_core()
            push(
                tb_rows(part, theirs + LATE, OWN - LATE, e), late_rows(part, 0, e), o_s.at[0], o_c.at[0], {"states": core}
            ).start()
            pltpu.make_async_copy(tb_rows(part, 0, ROWS, e), rows_of(part, c, slot[part], 0, ROWS, e), l_s.at[0]).start()
        for part in range(2):
            r = slice(part * ROWS, (part + 1) * ROWS)
            prec_b = tb[part, 1, :, e * H : (e + 1) * H]
            mean_f, prec_f = tb[part, 0, :, e * H : (e + 1) * H].astype(F32), prec_b.astype(F32)
            prod_f = (mean_f * prec_f).astype(BF16).astype(F32)
            co[e, r, 0:H] = (-2.0 * prod_f).astype(BF16)
            co[e, r, H:W] = prec_b
            term = jnp.sum(mean_f * prod_f - jnp.log(prec_f), axis=1, keepdims=True)
            if e == 0:
                cs[r, :] = jnp.broadcast_to(term, (ROWS, 128))
            else:
                cs[r, :] += jnp.broadcast_to(term, (ROWS, 128))

    nt = (((1,), (1,)), ((), ()))

    def rescore(e, n):
        f, ch = n // 2 % 2, 1 - c if n < 4 else c

        @pl.loop(n % 2 * 2, n % 2 * 2 + 2)
        def _(t):
            r = pl.ds(pl.multiple_of(t * 512, 512), 512)
            qt = lax.dot_general(co[e], xs[f, ch, r, e * W : (e + 1) * W], nt, preferred_element_type=F32)
            if e == 1:
                qt += jnp.concatenate([cs[...]] * 4, axis=1)
            v = jnp.sum(qt * post[f, ch, :, r].astype(F32), axis=0, keepdims=True)
            for i in range(4):
                s = t * 4 + i
                at_s = (ch, s if f == 0 else rev4(s), slice(f, f + 1), slice(None))
                part = v[:, i * 128 : (i + 1) * 128]
                qb[at_s] = part if e == 0 else qb[at_s] + part

    def q_push(i, src, dst, dev):
        push(src, dst, q_s.at[i], q_r.at[i], dev).start()

    def score_step(n):
        if n == 0:
            q_push(0, qb.at[1 - c], rq, {"states": core})
        elif n == 1:
            landed(rq, q_r.at[0])
            qy[...] = qb[c] + rq[...]
            for d in range(1, 4):
                q2 = (q + d) % 4
                q_push(1, qy.at[pl.ds(gray(q2) * 4, 4)], ry.at[d - 1], {"states": at(p, q2)})
        elif n == 2:
            landed(ry, q_r.at[1])
            qx[...] = qy[pl.ds(gray(q) * 4, 4)] + ry[0] + ry[1] + ry[2]
            for d in range(1, 4):
                p2 = (p + d) % 4
                q_push(2, qx.at[pl.ds(gray(p2), 1)], rx.at[d - 1], {"states": at(p2, q)})
        elif n == 3:
            landed(rx, q_r.at[2])
            q1[...] = qx[pl.ds(gray(p), 1)] + rx[0] + rx[1] + rx[2]
            for d in range(1, 4):
                q_push(3, q1, rh.at[d - 1], {"frames": (hi + d) % 4})
        else:
            landed(rh, q_r.at[3])
            quad = q1[0] + rh[0, 0] + rh[1, 0] + rh[2, 0]
            w_sum = jnp.sum(w_in[...].astype(BF16).astype(F32), axis=0, keepdims=True)
            for f in range(2):
                score_ref[f : f + 1, :] = -0.5 * quad[f : f + 1, :] / (D * w_sum[:, f * 128 : (f + 1) * 128])

    def outputs_here():
        landed(out.at[:, 0 : 32 * ROWS], o_c.at[0])
        landed(tb, l_s.at[0])

    def codes_start():
        gf.start(range(4))
        gf.start_core()

    do = {"G0": codes_start, "occ": occupancy, "OC": outputs_here}
    for h in range(5):
        if h:
            do[f"G{h}"] = lambda h=h: g_hop(h)
        do[f"GC{h}"] = lambda h=h: g_core(h)
        masks, n = HOPS[h], len(HOPS[h])
        pieces = (("", masks),) if n == 1 else (("0", masks[: n // 2]), ("1", masks[n // 2 :]))
        for tag, some in pieces:
            do[f"bo{h}{tag}"] = lambda some=some: build_all(c, slot[0], some)
            do[f"bc{h}{tag}"] = lambda some=some: build_all(1 - c, other[0], some)
    for e in range(2):
        do[f"Xs{e}a"] = lambda e=e: x_start(e, (0, 1))
        do[f"Xs{e}b"] = lambda e=e: x_start(e, (2, 3))
        do[f"XCs{e}"] = lambda e=e: x_start_core(e)
        for i in range(6):
            do[f"x{e}g{i}"] = lambda e=e, i=i: x_group(e, i)
            do[f"o{e}g{i}"] = lambda e=e, i=i: o_group(e, i)
            do[f"t{e}g{i}"] = lambda e=e, i=i: t_group(e, i)
        for i in range(3):
            do[f"XC{e}{i}"] = lambda e=e, i=i: x_core(e, i)
            do[f"U{e}{i}"] = lambda e=e, i=i: u_group(e, i)
        for mask in (0, 4, 8, 12):
            do[f"mo{mask}e{e}"] = lambda e=e, mask=mask: own_moments(mask, e)
            do[f"mc{mask}e{e}"] = lambda e=e, mask=mask: core_moments(mask, e)
        do[f"A{e}"] = lambda e=e: acc_send(e)
        do[f"AW{e}"] = lambda e=e: update(e)
        do[f"TW{e}"] = lambda e=e: table(e)
        for n in range(8):
            do[f"R{e}{n}"] = lambda e=e, n=n: rescore(e, n)
    for n in range(5):
        do[f"Q{n}"] = lambda n=n: score_step(n)

    with jax.named_scope("a0_barrier"):
        pl.semaphore_wait(barrier, 11)
    for n, name in enumerate(ORDER):
        with jax.named_scope(f"s{n:03d}_{name}"):
            do[name]()

    landed(g.at[0:31], g_s.at[0])
    landed(xs.at[:, :, 0:1984, 0:W], x_s.at[0])
    landed(out.at[:, 0 : 2 * (31 * OWN + 31 * LATE + 31 * (OWN - LATE))], o_s.at[0])
    landed(oc, oc_s.at[0])
    landed(racc, acc_s.at[0])
    landed(tb.at[:, :, 0:OWN], tb_s.at[0])
    landed(rq, q_s.at[0])
    landed(ry, q_s.at[1])
    landed(rx, q_s.at[2])
    landed(rh, q_s.at[3])


def per_device(features, state_ids, weights):
    hbm = pl.BlockSpec(memory_space=pltpu.HBM)
    place = pl.BlockSpec(memory_space=pl.ANY)
    vm = pl.BlockSpec(memory_space=pltpu.VMEM)
    dma = pltpu.SemaphoreType.DMA
    states = 64 * ROWS
    both, score = pl.pallas_call(
        kernel,
        out_shape=(
            pltpu.VMEM((2, states, W), BF16),
            pltpu.VMEM((2, 128), F32),
        ),
        in_specs=[hbm] * 3,
        out_specs=(place, vm),
        scratch_shapes=[
            pltpu.VMEM((256, W), BF16),
            pltpu.VMEM((32, 256), I32),
            pltpu.VMEM((32, 256), F32),
            pltpu.VMEM((2, 2, 2048, 2 * W), BF16),
            pltpu.VMEM((32, 64, 256), I16),
            pltpu.VMEM((2, 2, 2 * ROWS, 2048), BF16),
            pltpu.VMEM((2, 2 * ROWS, W), F32),
            pltpu.VMEM((2, 2, OWN, W), F32),
            pltpu.VMEM((2 * ROWS, 128), F32),
            pltpu.VMEM((8, 256), F32),
            pltpu.VMEM((8, 256), F32),
            pltpu.VMEM((256, 128), F32),
            pltpu.VMEM((2, 2, ROWS, W), BF16),
            pltpu.VMEM((2, 2 * ROWS, W), BF16),
            pltpu.VMEM((2 * ROWS, 128), F32),
            pltpu.VMEM((2, 16, 2, 128), F32),
            pltpu.VMEM((16, 2, 128), F32),
            pltpu.VMEM((16, 2, 128), F32),
            pltpu.VMEM((3, 4, 2, 128), F32),
            pltpu.VMEM((4, 2, 128), F32),
            pltpu.VMEM((3, 1, 2, 128), F32),
            pltpu.VMEM((1, 2, 128), F32),
            pltpu.VMEM((3, 1, 2, 128), F32),
            dma((3,)),
            dma((1,)), dma((4,)), dma((5,)),
            dma((1,)), dma((2, 6)), dma((2, 3)),
            dma((1,)), dma((2, 6)), dma((2, 6)), dma((2, 3)), dma((1,)),
            dma((1,)), dma((2,)),
            dma((1,)), dma((2,)),
            dma((1,)), dma((1,)),
            dma((1,)),
            dma((4,)), dma((4,)),
        ],
        compiler_params=pltpu.CompilerParams(
            collective_id=0, has_side_effects=True, vmem_limit_bytes=40 << 20
        ),
        name="fused",
    )(*[pltpu.with_memory_space_constraint(a, pltpu.HBM) for a in (features, state_ids.T, weights.T)])
    return both[0], both[1], score.reshape(-1)


def solution(mesh):
    return jax.shard_map(
        per_device,
        mesh=mesh,
        in_specs=(P("states", "frames"), P("states", None), P("states", None)),
        out_specs=(P(None, "frames"), P(None, "frames"), P("states")),
        check_vma=False,
    )
```

```python
import jax
import jax.numpy as jnp
from jax import lax
from jax.experimental import pallas as pl
from jax.experimental.pallas import tpu as pltpu
from jax.sharding import PartitionSpec as P

MESH = pl.DeviceIdType.MESH
F32, BF16, I16, I32 = jnp.float32, jnp.bfloat16, jnp.int16, jnp.int32
D = 1024
W = 256
ROWS = 96
OWN = 48
LATE = 32
FLOOR = 0.25
HOPS = ((0,), (1, 2, 4, 8), (3, 5, 6, 9, 10, 12), (7, 11, 13, 14), (15,))
GROUPS = ((1, 2), (4, 8), (3, 5, 6), (9, 10, 12), (7, 11, 13, 14), (15,))
LATER = ((1, 2, 4, 8), (3, 5, 6, 9, 10, 12), (7, 11, 13, 14, 15))

H = W // 2
ORDER = (
    "G0", "Xs0a", "Xs0b", "XCs0", "Xs1a", "Xs1b", "G1", "GC1", "x0g0", "bo11", "bc10", "GC0", "bo10", "x1g0", "x0g1",
    "bc0", "G2", "bo20", "bc11", "x0g2", "bo0", "bo21", "XCs1", "x1g1", "GC2", "bc20", "x0g3", "x1g2", "mo0e0",
    "bc21", "G3", "bo31", "x0g4", "XC00", "bo30", "GC3", "bc31", "mc0e0", "x1g3", "bc30", "G4", "XC01", "x1g4",
    "bo4", "mc4e0", "mc8e0", "x0g5", "mo12e0", "mo4e0", "GC4", "mo8e0", "bc4", "occ", "XC11", "XC02", "XC10",
    "mc12e0", "A0", "mo8e1", "mc4e1", "x1g5", "mo0e1", "mo4e1", "mo12e1", "mc8e1", "mc0e1", "XC12", "mc12e1", "A1",
    "AW0", "AW1", "o0g0", "TW0", "R03", "o0g1", "R00", "R02", "TW1", "o1g0", "R13", "R05", "o1g1", "R06", "R04",
    "o0g2", "R10", "R15", "R14", "t0g0", "R12", "t1g0", "U00", "R01", "o0g3", "R11", "R07", "R16", "Q0", "o1g2",
    "R17", "Q1", "o0g4", "t1g1", "U10", "o1g3", "t0g1", "t1g2", "t0g2", "Q2", "o1g4", "t1g3", "t0g3", "o0g5", "t0g4",
    "t1g4", "U01", "Q3", "U11", "o1g5", "t0g5", "t1g5", "U02", "U12", "Q4", "OC",
)


def flip(s, mask):
    for k in range(4):
        if mask >> k & 1:
            s = s + 2**k * (1 - 2 * ((s // 2**k) % 2))
    return s


def rev4(s):
    return (s % 2) * 8 + ((s // 2) % 2) * 4 + ((s // 4) % 2) * 2 + s // 8


def gray(r):
    return (r + r // 2) % 2 + 2 * (r // 2)


def place_of(groups, m):
    return [n for n, group in enumerate(groups) if m in group][0]


def landed(ref, sem):
    pltpu.make_async_copy(ref, ref, sem).wait()


def push(src, dst, send, recv, device):
    return pltpu.make_async_remote_copy(
        src_ref=src, dst_ref=dst, send_sem=send, recv_sem=recv, device_id=device, device_id_type=MESH
    )


class Flood:
    def __init__(self, view, slot, partners, core, c, send, recv, core_recv, first=None, up=None, up_view=None, up_recv=None):
        self.view, self.slot, self.partners, self.core, self.c = view, slot, partners, core, c
        self.send, self.recv, self.core_recv, self.first = send, recv, core_recv, first
        self.up, self.up_view, self.up_recv = up, up_view, up_recv

    def _pass(self, m, view, recv, device):
        dst = view(self.c, flip(self.slot, m))
        src = self.first if m == 0 and self.first is not None else dst
        push(src, dst, self.send, recv, {"states": device}).start()

    def start(self, ks):
        for k in ks:
            self._pass(0, self.view, self.recv(1 << k), self.partners[k])

    def start_core(self):
        self._pass(0, self.view, self.core_recv(0), self.core)

    def forward(self, m):
        for k in range(m.bit_length(), 4):
            self._pass(m, self.view, self.recv(m | 1 << k), self.partners[k])
        if self.up_view:
            self._pass(m, self.up_view, self.up_recv(m), self.up)
        self._pass(m, self.view, self.core_recv(m), self.core)


def kernel(
    x_hbm, ids_hbm, w_hbm, out, score_ref,
    x_in, ids_in, w_in, xs, g, post, acc, racc, occ, oc, roc, cnt, tb, co, cs, qb, rq, qy, ry, qx, rx, q1, rh,
    i_s, g_s, g_r, g_c, x_s, x_r, x_c, o_s, o_r, t_r, u_r, o_c, acc_s, acc_r, tb_s, tb_r, oc_s, oc_r, l_s, q_s, q_r,
):
    me = lax.axis_index("states")
    hi = lax.axis_index("frames")
    c = me % 2
    x = (me // 2) % 4
    y = (me // 8) % 4
    z = me // 32

    def device(z, y, x, c):
        return ((z * 4 + y) * 4 + x) * 2 + c

    p = x + c * (y - x)
    q = y + c * (x - y)

    def at(p2, q2):
        return device(z, q2 + c * (p2 - q2), p2 + c * (q2 - p2), c)

    v0, v1, v2, v3 = (p + p // 2) % 2, p // 2, (q + q // 2) % 2, q // 2
    near = [at(p + 1 - 2 * (p % 2), q), at(3 - p, q), at(p, q + 1 - 2 * (q % 2)), at(p, 3 - q)]
    core = device(z, y, x, 1 - c)
    up = device(1 - z, y, x, c)
    slot = (v0 + 2 * v1 + 4 * v2 + 8 * v3, v3 + 2 * v2 + 4 * v1 + 8 * v0)
    other = (v2 + 2 * v3 + 4 * v0 + 8 * v1, v1 + 2 * v0 + 4 * v3 + 8 * v2)

    barrier = pltpu.get_barrier_semaphore()
    for d in near + [at((p + 2) % 4, q), at(p, (q + 2) % 4), core, up]:
        pl.semaphore_signal(barrier, inc=1, device_id={"states": d}, device_id_type=MESH)
    for d in range(1, 4):
        pl.semaphore_signal(barrier, inc=1, device_id={"frames": (hi + d) % 4}, device_id_type=MESH)

    loads = [
        pltpu.make_async_copy(src, dst, i_s.at[i])
        for i, (src, dst) in enumerate(((ids_hbm, ids_in), (w_hbm, w_in), (x_hbm, x_in)))
    ]
    for cp in loads:
        cp.start()
    acc[...] = jnp.zeros_like(acc)
    occ[...] = jnp.zeros_like(occ)
    loads[0].wait()
    loads[1].wait()
    w_t = w_in[...].astype(BF16).astype(F32)
    g[c * 16 + slot[0], 0:32, :] = ids_in[...].astype(I16)
    g[c * 16 + slot[0], 32:64, :] = (w_t * 4096.0).astype(I32).astype(I16)
    loads[2].wait()
    for f in range(2):
        r = pl.ds(pl.multiple_of(slot[f] * 128, 128), 128)
        for e in range(2):
            xs[f, c, r, e * W : e * W + H] = x_in[f * 128 : (f + 1) * 128, e * H : (e + 1) * H]

    base = [pl.multiple_of(((c * 2 + part) * 16 + slot[part]) * ROWS, ROWS) for part in range(2)]
    iota = lax.broadcasted_iota(I32, (ROWS, 128), 0)
    rows = jnp.concatenate([(iota + base[0]).astype(I16), (iota + base[1]).astype(I16)], axis=0)

    def build(ch, s):
        ids = g[ch * 16 + s, 0:32, :].astype(I32)
        wv = g[ch * 16 + s, 32:64, :].astype(I32).astype(F32) * (1.0 / 4096.0)
        for f in range(2):
            lanes = slice(f * 128, (f + 1) * 128)
            block = jnp.zeros((2 * ROWS, 128), BF16)
            for j in range(32):
                idj = jnp.broadcast_to(ids[j : j + 1, lanes].astype(I16), (2 * ROWS, 128))
                wj = jnp.broadcast_to(wv[j : j + 1, lanes].astype(BF16), (2 * ROWS, 128))
                block = jnp.where(rows == idj, wj, block)
            col = pl.multiple_of((s if f == 0 else rev4(s)) * 128, 128)
            post[f, ch, :, pl.ds(col, 128)] = block
            occ[...] += block.astype(F32)

    def build_all(ch, first, masks):
        if len(masks) == 1:
            return build(ch, flip(first, masks[0]))

        def body(_, left):
            s = first
            for k in range(4):
                s = s + 2**k * ((left // 2**k) % 2) * (1 - 2 * ((first // 2**k) % 2))
            build(ch, s)
            return left // 16

        lax.fori_loop(0, len(masks), body, jnp.int32(sum(m << 4 * i for i, m in enumerate(masks))))

    def moments(f, ch, b, e):
        r = pl.ds(pl.multiple_of(b * 512, 512), 512)
        xw = xs[f, ch, r, e * W : e * W + H].astype(F32)
        xs[f, ch, r, e * W + H : (e + 1) * W] = (xw * xw).astype(BF16)
        acc[e] += jnp.dot(post[f, ch, :, r], xs[f, ch, r, e * W : (e + 1) * W], preferred_element_type=F32)

    orders = (near, near[::-1])
    gf = Flood(
        lambda r, s: g.at[r * 16 + s], slot[0], near, core, c, g_s.at[0],
        lambda m: g_r.at[place_of(HOPS, m) - 1], lambda m: g_c.at[place_of(HOPS, m)],
    )
    xf = [
        [
            Flood(
                lambda r, s, f=f, e=e: xs.at[f, r, pl.ds(pl.multiple_of(s * 128, 128), 128), e * W : e * W + H],
                slot[f], orders[f], core, c, x_s.at[0],
                lambda m, e=e: x_r.at[e, place_of(GROUPS, m)], lambda m, e=e: x_c.at[e, max(m.bit_count(), 2) - 2],
            )
            for f in range(2)
        ]
        for e in range(2)
    ]

    def g_hop(h):
        landed(g.at[0 : len(HOPS[h])], g_r.at[h - 1])
        for m in HOPS[h]:
            gf.forward(m)

    def g_core(h):
        landed(g.at[0 : len(HOPS[h])], g_c.at[h])

    def x_start(e, ks):
        for f in range(2):
            xf[e][f].start(ks)

    def x_start_core(e):
        for f in range(2):
            xf[e][f].start_core()

    def x_group(e, i):
        landed(xs.at[0, 0, 0 : len(GROUPS[i]) * 256, 0:H], x_r.at[e, i])
        for m in GROUPS[i]:
            for f in range(2):
                xf[e][f].forward(m)

    def x_core(e, i):
        landed(xs.at[:, 0, 0 : (11, 4, 1)[i] * 128, 0:H], x_c.at[e, i])

    def own_moments(mask, e):
        for f in range(2):
            moments(f, c, flip(slot[f], mask) // 4, e)

    def core_moments(mask, e):
        for f in range(2):
            moments(f, 1 - c, flip(other[f], mask) // 4, e)

    def up_push(src, dst, send, recv):
        push(src, dst, send, recv, {"states": up}).start()

    def occupancy():
        oc[...] = jnp.zeros_like(oc)
        oc[0:1, 0:192] = jnp.sum(jnp.transpose(occ[...]), axis=0, keepdims=True)
        up_push(oc, roc, oc_s.at[0], oc_r.at[0])

    def acc_send(e):
        for part in range(2):
            r = pl.ds(pl.multiple_of(part * ROWS + (1 - z) * OWN, 8), OWN)
            up_push(acc.at[e, r], racc.at[e, part], acc_s.at[0], acc_r.at[e])

    def rows_of(part, r, s, first, n, e):
        start = pl.multiple_of(((r * 2 + part) * 16 + s) * ROWS + first, 16)
        return out.at[:, pl.ds(start, n), e * H : (e + 1) * H]

    def tb_rows(part, first, n, e):
        return tb.at[part, :, pl.ds(pl.multiple_of(first, 16), n), e * H : (e + 1) * H]

    mine, theirs = z * OWN, (1 - z) * OWN
    of, tf = [[], []], [[], []]
    for e in range(2):
        for t in range(2):
            of[e].append(
                Flood(
                    lambda r, s, t=t, e=e: rows_of(t, r, s, mine, OWN, e), slot[t], orders[t], core, c, o_s.at[0],
                    lambda m, e=e: o_r.at[e, place_of(GROUPS, m)], lambda m: o_c.at[0], tb_rows(t, mine, OWN, e),
                    up, lambda r, s, t=t, e=e: rows_of(t, r, s, mine + LATE, OWN - LATE, e),
                    lambda m, e=e: u_r.at[e, place_of(LATER, m)],
                )
            )
            tf[e].append(
                Flood(
                    lambda r, s, t=t, e=e: rows_of(t, r, s, theirs, LATE, e), slot[t], orders[t], core, c, o_s.at[0],
                    lambda m, e=e: t_r.at[e, place_of(GROUPS, m)], lambda m: o_c.at[0], tb_rows(t, theirs, LATE, e),
                )
            )

    def o_group(e, i):
        landed(out.at[:, 0 : len(GROUPS[i]) * 2 * OWN, 0:H], o_r.at[e, i])
        for m in GROUPS[i]:
            for t in range(2):
                of[e][t].forward(m)

    def t_group(e, i):
        landed(out.at[:, 0 : len(GROUPS[i]) * 2 * LATE, 0:H], t_r.at[e, i])
        for m in GROUPS[i]:
            for t in range(2):
                tf[e][t].forward(m)

    def late_rows(t, m, e):
        return rows_of(t, c, flip(slot[t], m), theirs + LATE, OWN - LATE, e)

    def u_group(e, i):
        landed(out.at[:, 0 : len(LATER[i]) * 2 * (OWN - LATE), 0:H], u_r.at[e, i])
        for m in LATER[i]:
            for t in range(2):
                push(late_rows(t, m, e), late_rows(t, m, e), o_s.at[0], o_c.at[0], {"states": core}).start()

    def update(e):
        landed(racc.at[e], acc_r.at[e])
        if e == 0:
            landed(roc, oc_r.at[0])
            cnt[...] = jnp.transpose(jnp.broadcast_to(oc[0:1, :] + roc[0:1, :], (128, 256)))
        own = pl.ds(pl.multiple_of(mine, 16), OWN)
        for part in range(2):
            r = pl.ds(pl.multiple_of(part * ROWS + z * OWN, 8), OWN)
            total = acc[e, r, :] + racc[e, part]
            count = cnt[r, :]
            mean = total[:, 0:H] / count
            var = jnp.maximum(total[:, H:W] / count - mean * mean, FLOOR)
            tb[part, 0, own, e * H : (e + 1) * H] = mean.astype(BF16)
            tb[part, 1, own, e * H : (e + 1) * H] = (1.0 / var).astype(BF16)
        for part in range(2):
            up_push(tb_rows(part, mine, OWN, e), tb_rows(part, mine, OWN, e), tb_s.at[0], tb_r.at[e])
        for ks in ((0, 1), (2, 3)):
            for part in range(2):
                of[e][part].start(ks)
        for part in range(2):
            of[e][part].start_core()

    def table(e):
        landed(tb.at[:, :, 0:OWN, 0:H], tb_r.at[e])
        for ks in ((0, 1), (2, 3)):
            for part in range(2):
                tf[e][part].start(ks)
        for part in range(2):
            tf[e][part].start_core()
            push(
                tb_rows(part, theirs + LATE, OWN - LATE, e), late_rows(part, 0, e), o_s.at[0], o_c.at[0], {"states": core}
            ).start()
            pltpu.make_async_copy(tb_rows(part, 0, ROWS, e), rows_of(part, c, slot[part], 0, ROWS, e), l_s.at[0]).start()
        for part in range(2):
            r = slice(part * ROWS, (part + 1) * ROWS)
            prec_b = tb[part, 1, :, e * H : (e + 1) * H]
            mean_f, prec_f = tb[part, 0, :, e * H : (e + 1) * H].astype(F32), prec_b.astype(F32)
            prod_f = (mean_f * prec_f).astype(BF16).astype(F32)
            co[e, r, 0:H] = (-2.0 * prod_f).astype(BF16)
            co[e, r, H:W] = prec_b
            term = jnp.sum(mean_f * prod_f - jnp.log(prec_f), axis=1, keepdims=True)
            if e == 0:
                cs[r, :] = jnp.broadcast_to(term, (ROWS, 128))
            else:
                cs[r, :] += jnp.broadcast_to(term, (ROWS, 128))

    nt = (((1,), (1,)), ((), ()))

    def rescore(e, n):
        f, ch = n // 2 % 2, 1 - c if n < 4 else c

        for t in range(n % 2 * 2, n % 2 * 2 + 2):
            r = pl.ds(t * 512, 512)
            qt = lax.dot_general(co[e], xs[f, ch, r, e * W : (e + 1) * W], nt, preferred_element_type=F32)
            if e == 1:
                qt += jnp.concatenate([cs[...]] * 4, axis=1)
            v = jnp.sum(qt * post[f, ch, :, r].astype(F32), axis=0, keepdims=True)
            for i in range(4):
                s = t * 4 + i
                at_s = (ch, s if f == 0 else rev4(s), slice(f, f + 1), slice(None))
                part = v[:, i * 128 : (i + 1) * 128]
                qb[at_s] = part if e == 0 else qb[at_s] + part

    def q_push(i, src, dst, dev):
        push(src, dst, q_s.at[i], q_r.at[i], dev).start()

    def score_step(n):
        if n == 0:
            q_push(0, qb.at[1 - c], rq, {"states": core})
        elif n == 1:
            landed(rq, q_r.at[0])
            qy[...] = qb[c] + rq[...]
            for d in range(1, 4):
                q2 = (q + d) % 4
                q_push(1, qy.at[pl.ds(gray(q2) * 4, 4)], ry.at[d - 1], {"states": at(p, q2)})
        elif n == 2:
            landed(ry, q_r.at[1])
            qx[...] = qy[pl.ds(gray(q) * 4, 4)] + ry[0] + ry[1] + ry[2]
            for d in range(1, 4):
                p2 = (p + d) % 4
                q_push(2, qx.at[pl.ds(gray(p2), 1)], rx.at[d - 1], {"states": at(p2, q)})
        elif n == 3:
            landed(rx, q_r.at[2])
            q1[...] = qx[pl.ds(gray(p), 1)] + rx[0] + rx[1] + rx[2]
            for d in range(1, 4):
                q_push(3, q1, rh.at[d - 1], {"frames": (hi + d) % 4})
        else:
            landed(rh, q_r.at[3])
            quad = q1[0] + rh[0, 0] + rh[1, 0] + rh[2, 0]
            w_sum = jnp.sum(w_in[...].astype(BF16).astype(F32), axis=0, keepdims=True)
            for f in range(2):
                score_ref[f : f + 1, :] = -0.5 * quad[f : f + 1, :] / (D * w_sum[:, f * 128 : (f + 1) * 128])

    def outputs_here():
        landed(out.at[:, 0 : 32 * ROWS], o_c.at[0])
        landed(tb, l_s.at[0])

    def codes_start():
        gf.start(range(4))
        gf.start_core()

    do = {"G0": codes_start, "occ": occupancy, "OC": outputs_here}
    for h in range(5):
        if h:
            do[f"G{h}"] = lambda h=h: g_hop(h)
        do[f"GC{h}"] = lambda h=h: g_core(h)
        masks, n = HOPS[h], len(HOPS[h])
        pieces = (("", masks),) if n == 1 else (("0", masks[: n // 2]), ("1", masks[n // 2 :]))
        for tag, some in pieces:
            do[f"bo{h}{tag}"] = lambda some=some: build_all(c, slot[0], some)
            do[f"bc{h}{tag}"] = lambda some=some: build_all(1 - c, other[0], some)
    for e in range(2):
        do[f"Xs{e}a"] = lambda e=e: x_start(e, (0, 1))
        do[f"Xs{e}b"] = lambda e=e: x_start(e, (2, 3))
        do[f"XCs{e}"] = lambda e=e: x_start_core(e)
        for i in range(6):
            do[f"x{e}g{i}"] = lambda e=e, i=i: x_group(e, i)
            do[f"o{e}g{i}"] = lambda e=e, i=i: o_group(e, i)
            do[f"t{e}g{i}"] = lambda e=e, i=i: t_group(e, i)
        for i in range(3):
            do[f"XC{e}{i}"] = lambda e=e, i=i: x_core(e, i)
            do[f"U{e}{i}"] = lambda e=e, i=i: u_group(e, i)
        for mask in (0, 4, 8, 12):
            do[f"mo{mask}e{e}"] = lambda e=e, mask=mask: own_moments(mask, e)
            do[f"mc{mask}e{e}"] = lambda e=e, mask=mask: core_moments(mask, e)
        do[f"A{e}"] = lambda e=e: acc_send(e)
        do[f"AW{e}"] = lambda e=e: update(e)
        do[f"TW{e}"] = lambda e=e: table(e)
        for n in range(8):
            do[f"R{e}{n}"] = lambda e=e, n=n: rescore(e, n)
    for n in range(5):
        do[f"Q{n}"] = lambda n=n: score_step(n)

    with jax.named_scope("a0_barrier"):
        pl.semaphore_wait(barrier, 11)
    for n, name in enumerate(ORDER):
        with jax.named_scope(f"s{n:03d}_{name}"):
            do[name]()

    landed(g.at[0:31], g_s.at[0])
    landed(xs.at[:, :, 0:1984, 0:W], x_s.at[0])
    landed(out.at[:, 0 : 2 * (31 * OWN + 31 * LATE + 31 * (OWN - LATE))], o_s.at[0])
    landed(oc, oc_s.at[0])
    landed(racc, acc_s.at[0])
    landed(tb.at[:, :, 0:OWN], tb_s.at[0])
    landed(rq, q_s.at[0])
    landed(ry, q_s.at[1])
    landed(rx, q_s.at[2])
    landed(rh, q_s.at[3])


def per_device(features, state_ids, weights):
    hbm = pl.BlockSpec(memory_space=pltpu.HBM)
    place = pl.BlockSpec(memory_space=pl.ANY)
    vm = pl.BlockSpec(memory_space=pltpu.VMEM)
    dma = pltpu.SemaphoreType.DMA
    states = 64 * ROWS
    both, score = pl.pallas_call(
        kernel,
        out_shape=(
            pltpu.VMEM((2, states, W), BF16),
            pltpu.VMEM((2, 128), F32),
        ),
        in_specs=[hbm] * 3,
        out_specs=(place, vm),
        scratch_shapes=[
            pltpu.VMEM((256, W), BF16),
            pltpu.VMEM((32, 256), I32),
            pltpu.VMEM((32, 256), F32),
            pltpu.VMEM((2, 2, 2048, 2 * W), BF16),
            pltpu.VMEM((32, 64, 256), I16),
            pltpu.VMEM((2, 2, 2 * ROWS, 2048), BF16),
            pltpu.VMEM((2, 2 * ROWS, W), F32),
            pltpu.VMEM((2, 2, OWN, W), F32),
            pltpu.VMEM((2 * ROWS, 128), F32),
            pltpu.VMEM((8, 256), F32),
            pltpu.VMEM((8, 256), F32),
            pltpu.VMEM((256, 128), F32),
            pltpu.VMEM((2, 2, ROWS, W), BF16),
            pltpu.VMEM((2, 2 * ROWS, W), BF16),
            pltpu.VMEM((2 * ROWS, 128), F32),
            pltpu.VMEM((2, 16, 2, 128), F32),
            pltpu.VMEM((16, 2, 128), F32),
            pltpu.VMEM((16, 2, 128), F32),
            pltpu.VMEM((3, 4, 2, 128), F32),
            pltpu.VMEM((4, 2, 128), F32),
            pltpu.VMEM((3, 1, 2, 128), F32),
            pltpu.VMEM((1, 2, 128), F32),
            pltpu.VMEM((3, 1, 2, 128), F32),
            dma((3,)),
            dma((1,)), dma((4,)), dma((5,)),
            dma((1,)), dma((2, 6)), dma((2, 3)),
            dma((1,)), dma((2, 6)), dma((2, 6)), dma((2, 3)), dma((1,)),
            dma((1,)), dma((2,)),
            dma((1,)), dma((2,)),
            dma((1,)), dma((1,)),
            dma((1,)),
            dma((4,)), dma((4,)),
        ],
        compiler_params=pltpu.CompilerParams(
            collective_id=0, has_side_effects=True, vmem_limit_bytes=40 << 20
        ),
        name="fused",
    )(*[pltpu.with_memory_space_constraint(a, pltpu.HBM) for a in (features, state_ids.T, weights.T)])
    return both[0], both[1], score.reshape(-1)


def solution(mesh):
    return jax.shard_map(
        per_device,
        mesh=mesh,
        in_specs=(P("states", "frames"), P("states", None), P("states", None)),
        out_specs=(P(None, "frames"), P(None, "frames"), P("states")),
        check_vma=False,
    )
```

```python
import jax
import jax.numpy as jnp
from jax import lax
from jax.experimental import pallas as pl
from jax.experimental.pallas import tpu as pltpu
from jax.sharding import PartitionSpec as P

MESH = pl.DeviceIdType.MESH
F32, BF16, I16, I32 = jnp.float32, jnp.bfloat16, jnp.int16, jnp.int32
D = 1024
W = 256
ROWS = 96
OWN = 48
LATE = 32
FLOOR = 0.25
PIECES = 4
HOPS = ((0,), (1, 2, 4, 8), (3, 5, 6, 9, 10, 12), (7, 11, 13, 14), (15,))
GROUPS = ((1, 2), (4, 8), (3, 5, 6), (9, 10, 12), (7, 11, 13, 14), (15,))
LATER = ((1, 2, 4, 8), (3, 5, 6, 9, 10, 12), (7, 11, 13, 14, 15))

H = W // 2
ORDER = (
    "G0", "Xs0a", "Xs0b", "XCs0", "Xs1a", "Xs1b", "G1", "GC1", "x0g0", "bo11", "bc10", "GC0", "bo10", "x1g0", "x0g1",
    "bc0", "G2", "bo20", "bc11", "x0g2", "bo0", "bo21", "XCs1", "x1g1", "GC2", "bc20", "x0g3", "x1g2", "mo0e0",
    "bc21", "G3", "bo31", "x0g4", "XC00", "bo30", "GC3", "bc31", "mc0e0", "x1g3", "bc30", "G4", "XC01", "x1g4",
    "bo4", "mc4e0", "mc8e0", "x0g5", "mo12e0", "mo4e0", "GC4", "mo8e0", "bc4", "occ", "XC11", "XC02", "XC10",
    "mc12e0", "A0", "mo8e1", "mc4e1", "x1g5", "mo0e1", "mo4e1", "mo12e1", "mc8e1", "mc0e1", "XC12", "mc12e1", "A1",
    "AW0", "AW1", "o0g0", "TW0", "R03", "o0g1", "R00", "R02", "TW1", "o1g0", "R13", "R05", "o1g1", "R06", "R04",
    "o0g2", "R10", "R15", "R14", "t0g0", "R12", "t1g0", "U00", "R01", "o0g3", "R11", "R07", "R16", "Q0", "o1g2",
    "R17", "Q1", "o0g4", "t1g1", "U10", "o1g3", "t0g1", "t1g2", "t0g2", "Q2", "o1g4", "t1g3", "t0g3", "o0g5", "t0g4",
    "t1g4", "U01", "Q3", "U11", "o1g5", "t0g5", "t1g5", "U02", "U12", "Q4", "OC",
)


def flip(s, mask):
    for k in range(4):
        if mask >> k & 1:
            s = s + 2**k * (1 - 2 * ((s // 2**k) % 2))
    return s


def rev4(s):
    return (s % 2) * 8 + ((s // 2) % 2) * 4 + ((s // 4) % 2) * 2 + s // 8


def gray(r):
    return (r + r // 2) % 2 + 2 * (r // 2)


def place_of(groups, m):
    return [n for n, group in enumerate(groups) if m in group][0]


def landed(ref, sem):
    pltpu.make_async_copy(ref, ref, sem).wait()


def push(src, dst, send, recv, device):
    return pltpu.make_async_remote_copy(
        src_ref=src, dst_ref=dst, send_sem=send, recv_sem=recv, device_id=device, device_id_type=MESH
    )


class Flood:
    def __init__(self, view, slot, partners, core, c, send, recv, core_recv, first=None, up=None, up_view=None, up_recv=None):
        self.view, self.slot, self.partners, self.core, self.c = view, slot, partners, core, c
        self.send, self.recv, self.core_recv, self.first = send, recv, core_recv, first
        self.up, self.up_view, self.up_recv = up, up_view, up_recv

    def _pass(self, m, view, recv, device):
        dst = view(self.c, flip(self.slot, m))
        src = self.first if m == 0 and self.first is not None else dst
        push(src, dst, self.send, recv, {"states": device}).start()

    def start(self, ks):
        for k in ks:
            self._pass(0, self.view, self.recv(1 << k), self.partners[k])

    def start_core(self):
        self._pass(0, self.view, self.core_recv(0), self.core)

    def forward(self, m):
        for k in range(m.bit_length(), 4):
            self._pass(m, self.view, self.recv(m | 1 << k), self.partners[k])
        if self.up_view:
            self._pass(m, self.up_view, self.up_recv(m), self.up)
        self._pass(m, self.view, self.core_recv(m), self.core)


def kernel(
    x_hbm, ids_hbm, w_hbm, out, score_ref,
    x_in, ids_in, w_in, xs, g, post, acc, racc, occ, oc, roc, cnt, tb, co, cs, qb, rq, qy, ry, qx, rx, q1, rh,
    i_s, g_s, g_r, g_c, x_s, x_r, x_c, o_s, o_r, t_r, u_r, o_c, acc_s, acc_r, tb_s, tb_r, oc_s, oc_r, l_s, q_s, q_r,
):
    me = lax.axis_index("states")
    hi = lax.axis_index("frames")
    c = me % 2
    x = (me // 2) % 4
    y = (me // 8) % 4
    z = me // 32

    def device(z, y, x, c):
        return ((z * 4 + y) * 4 + x) * 2 + c

    p = x + c * (y - x)
    q = y + c * (x - y)

    def at(p2, q2):
        return device(z, q2 + c * (p2 - q2), p2 + c * (q2 - p2), c)

    v0, v1, v2, v3 = (p + p // 2) % 2, p // 2, (q + q // 2) % 2, q // 2
    near = [at(p + 1 - 2 * (p % 2), q), at(3 - p, q), at(p, q + 1 - 2 * (q % 2)), at(p, 3 - q)]
    core = device(z, y, x, 1 - c)
    up = device(1 - z, y, x, c)
    slot = (v0 + 2 * v1 + 4 * v2 + 8 * v3, v3 + 2 * v2 + 4 * v1 + 8 * v0)
    other = (v2 + 2 * v3 + 4 * v0 + 8 * v1, v1 + 2 * v0 + 4 * v3 + 8 * v2)

    barrier = pltpu.get_barrier_semaphore()
    for d in near + [at((p + 2) % 4, q), at(p, (q + 2) % 4), core, up]:
        pl.semaphore_signal(barrier, inc=1, device_id={"states": d}, device_id_type=MESH)
    for d in range(1, 4):
        pl.semaphore_signal(barrier, inc=1, device_id={"frames": (hi + d) % 4}, device_id_type=MESH)

    loads = [
        pltpu.make_async_copy(src, dst, i_s.at[i])
        for i, (src, dst) in enumerate(((ids_hbm, ids_in), (w_hbm, w_in), (x_hbm, x_in)))
    ]
    for cp in loads:
        cp.start()
    acc[...] = jnp.zeros_like(acc)
    occ[...] = jnp.zeros_like(occ)
    loads[0].wait()
    loads[1].wait()
    w_t = w_in[...].astype(BF16).astype(F32)
    g[c * 16 + slot[0], 0:32, :] = ids_in[...].astype(I16)
    g[c * 16 + slot[0], 32:64, :] = (w_t * 4096.0).astype(I32).astype(I16)
    loads[2].wait()
    for f in range(2):
        r = pl.ds(pl.multiple_of(slot[f] * 128, 128), 128)
        for e in range(2):
            xs[f, c, r, e * W : e * W + H] = x_in[f * 128 : (f + 1) * 128, e * H : (e + 1) * H]

    base = [pl.multiple_of(((c * 2 + part) * 16 + slot[part]) * ROWS, ROWS) for part in range(2)]
    iota = lax.broadcasted_iota(I32, (ROWS, 128), 0)
    rows = jnp.concatenate([(iota + base[0]).astype(I16), (iota + base[1]).astype(I16)], axis=0)

    def build(ch, s):
        ids = g[ch * 16 + s, 0:32, :].astype(I32)
        wv = g[ch * 16 + s, 32:64, :].astype(I32).astype(F32) * (1.0 / 4096.0)
        for f in range(2):
            lanes = slice(f * 128, (f + 1) * 128)
            block = jnp.zeros((2 * ROWS, 128), BF16)
            for j in range(32):
                idj = jnp.broadcast_to(ids[j : j + 1, lanes].astype(I16), (2 * ROWS, 128))
                wj = jnp.broadcast_to(wv[j : j + 1, lanes].astype(BF16), (2 * ROWS, 128))
                block = jnp.where(rows == idj, wj, block)
            col = pl.multiple_of((s if f == 0 else rev4(s)) * 128, 128)
            post[f, ch, :, pl.ds(col, 128)] = block
            occ[...] += block.astype(F32)

    def build_all(ch, first, masks):
        if len(masks) == 1:
            return build(ch, flip(first, masks[0]))

        def body(_, left):
            s = first
            for k in range(4):
                s = s + 2**k * ((left // 2**k) % 2) * (1 - 2 * ((first // 2**k) % 2))
            build(ch, s)
            return left // 16

        lax.fori_loop(0, len(masks), body, jnp.int32(sum(m << 4 * i for i, m in enumerate(masks))))

    def moments(f, ch, b, e):
        r = pl.ds(pl.multiple_of(b * 512, 512), 512)
        xw = xs[f, ch, r, e * W : e * W + H].astype(F32)
        xs[f, ch, r, e * W + H : (e + 1) * W] = (xw * xw).astype(BF16)
        acc[e] += jnp.dot(post[f, ch, :, r], xs[f, ch, r, e * W : (e + 1) * W], preferred_element_type=F32)

    orders = (near, near[::-1])
    gf = Flood(
        lambda r, s: g.at[r * 16 + s], slot[0], near, core, c, g_s.at[0],
        lambda m: g_r.at[place_of(HOPS, m) - 1], lambda m: g_c.at[place_of(HOPS, m)],
    )
    xf = [
        [
            Flood(
                lambda r, s, f=f, e=e: xs.at[f, r, pl.ds(pl.multiple_of(s * 128, 128), 128), e * W : e * W + H],
                slot[f], orders[f], core, c, x_s.at[0],
                lambda m, e=e: x_r.at[e, place_of(GROUPS, m)], lambda m, e=e: x_c.at[e, max(m.bit_count(), 2) - 2],
            )
            for f in range(2)
        ]
        for e in range(2)
    ]

    def g_hop(h):
        landed(g.at[0 : len(HOPS[h])], g_r.at[h - 1])
        for m in HOPS[h]:
            gf.forward(m)

    def g_core(h):
        landed(g.at[0 : len(HOPS[h])], g_c.at[h])

    def x_start(e, ks):
        for f in range(2):
            xf[e][f].start(ks)

    def x_start_core(e):
        for f in range(2):
            xf[e][f].start_core()

    def x_group(e, i):
        landed(xs.at[0, 0, 0 : len(GROUPS[i]) * 256, 0:H], x_r.at[e, i])
        for m in GROUPS[i]:
            for f in range(2):
                xf[e][f].forward(m)

    def x_core(e, i):
        landed(xs.at[:, 0, 0 : (11, 4, 1)[i] * 128, 0:H], x_c.at[e, i])

    def own_moments(mask, e):
        for f in range(2):
            moments(f, c, flip(slot[f], mask) // 4, e)

    def core_moments(mask, e):
        for f in range(2):
            moments(f, 1 - c, flip(other[f], mask) // 4, e)

    def up_push(src, dst, send, recv):
        push(src, dst, send, recv, {"states": up}).start()

    def occupancy():
        oc[...] = jnp.zeros_like(oc)
        oc[0:1, 0:192] = jnp.sum(jnp.transpose(occ[...]), axis=0, keepdims=True)
        up_push(oc, roc, oc_s.at[0], oc_r.at[0])

    def acc_send(e):
        for part in range(2):
            r = pl.ds(pl.multiple_of(part * ROWS + (1 - z) * OWN, 8), OWN)
            up_push(acc.at[e, r], racc.at[e, part], acc_s.at[0], acc_r.at[e])

    def rows_of(part, r, s, first, n, e):
        start = pl.multiple_of(((r * 2 + part) * 16 + s) * ROWS + first, 16)
        return out.at[:, pl.ds(start, n), e * H : (e + 1) * H]

    def tb_rows(part, first, n, e):
        return tb.at[part, :, pl.ds(pl.multiple_of(first, 16), n), e * H : (e + 1) * H]

    mine, theirs = z * OWN, (1 - z) * OWN
    of, tf = [[], []], [[], []]
    for e in range(2):
        for t in range(2):
            of[e].append(
                Flood(
                    lambda r, s, t=t, e=e: rows_of(t, r, s, mine, OWN, e), slot[t], orders[t], core, c, o_s.at[0],
                    lambda m, e=e: o_r.at[e, place_of(GROUPS, m)], lambda m: o_c.at[0], tb_rows(t, mine, OWN, e),
                    up, lambda r, s, t=t, e=e: rows_of(t, r, s, mine + LATE, OWN - LATE, e),
                    lambda m, e=e: u_r.at[e, place_of(LATER, m)],
                )
            )
            tf[e].append(
                Flood(
                    lambda r, s, t=t, e=e: rows_of(t, r, s, theirs, LATE, e), slot[t], orders[t], core, c, o_s.at[0],
                    lambda m, e=e: t_r.at[e, place_of(GROUPS, m)], lambda m: o_c.at[0], tb_rows(t, theirs, LATE, e),
                )
            )

    def o_group(e, i):
        landed(out.at[:, 0 : len(GROUPS[i]) * 2 * OWN, 0:H], o_r.at[e, i])
        for m in GROUPS[i]:
            for t in range(2):
                of[e][t].forward(m)

    def t_group(e, i):
        landed(out.at[:, 0 : len(GROUPS[i]) * 2 * LATE, 0:H], t_r.at[e, i])
        for m in GROUPS[i]:
            for t in range(2):
                tf[e][t].forward(m)

    def late_rows(t, m, e):
        return rows_of(t, c, flip(slot[t], m), theirs + LATE, OWN - LATE, e)

    def u_group(e, i):
        landed(out.at[:, 0 : len(LATER[i]) * 2 * (OWN - LATE), 0:H], u_r.at[e, i])
        for m in LATER[i]:
            for t in range(2):
                push(late_rows(t, m, e), late_rows(t, m, e), o_s.at[0], o_c.at[0], {"states": core}).start()

    def update(e):
        landed(racc.at[e], acc_r.at[e])
        if e == 0:
            landed(roc, oc_r.at[0])
            cnt[...] = jnp.transpose(jnp.broadcast_to(oc[0:1, :] + roc[0:1, :], (128, 256)))
        own = pl.ds(pl.multiple_of(mine, 16), OWN)
        for part in range(2):
            r = pl.ds(pl.multiple_of(part * ROWS + z * OWN, 8), OWN)
            total = acc[e, r, :] + racc[e, part]
            count = cnt[r, :]
            mean = total[:, 0:H] / count
            var = jnp.maximum(total[:, H:W] / count - mean * mean, FLOOR)
            tb[part, 0, own, e * H : (e + 1) * H] = mean.astype(BF16)
            tb[part, 1, own, e * H : (e + 1) * H] = (1.0 / var).astype(BF16)
        for part in range(2):
            up_push(tb_rows(part, mine, OWN, e), tb_rows(part, mine, OWN, e), tb_s.at[0], tb_r.at[e])
        for ks in ((0, 1), (2, 3)):
            for part in range(2):
                of[e][part].start(ks)
        for part in range(2):
            of[e][part].start_core()

    def table(e):
        landed(tb.at[:, :, 0:OWN, 0:H], tb_r.at[e])
        for ks in ((0, 1), (2, 3)):
            for part in range(2):
                tf[e][part].start(ks)
        for part in range(2):
            tf[e][part].start_core()
            push(
                tb_rows(part, theirs + LATE, OWN - LATE, e), late_rows(part, 0, e), o_s.at[0], o_c.at[0], {"states": core}
            ).start()
            pltpu.make_async_copy(tb_rows(part, 0, ROWS, e), rows_of(part, c, slot[part], 0, ROWS, e), l_s.at[0]).start()
        for part in range(2):
            r = slice(part * ROWS, (part + 1) * ROWS)
            prec_b = tb[part, 1, :, e * H : (e + 1) * H]
            mean_f, prec_f = tb[part, 0, :, e * H : (e + 1) * H].astype(F32), prec_b.astype(F32)
            prod_f = (mean_f * prec_f).astype(BF16).astype(F32)
            co[e, r, 0:H] = (-2.0 * prod_f).astype(BF16)
            co[e, r, H:W] = prec_b
            term = jnp.sum(mean_f * prod_f - jnp.log(prec_f), axis=1, keepdims=True)
            if e == 0:
                cs[r, :] = jnp.broadcast_to(term, (ROWS, 128))
            else:
                cs[r, :] += jnp.broadcast_to(term, (ROWS, 128))

    nt = (((1,), (1,)), ((), ()))

    def rescore(e, n):
        f, ch = n // 2 % 2, 1 - c if n < 4 else c

        for t in range(n % 2 * 2, n % 2 * 2 + 2):
            r = pl.ds(t * 512, 512)
            qt = lax.dot_general(co[e], xs[f, ch, r, e * W : (e + 1) * W], nt, preferred_element_type=F32)
            if e == 1:
                qt += jnp.concatenate([cs[...]] * 4, axis=1)
            v = jnp.sum(qt * post[f, ch, :, r].astype(F32), axis=0, keepdims=True)
            for i in range(4):
                s = t * 4 + i
                at_s = (ch, s if f == 0 else rev4(s), slice(f, f + 1), slice(None))
                part = v[:, i * 128 : (i + 1) * 128]
                qb[at_s] = part if e == 0 else qb[at_s] + part

    def q_push(i, src, dst, dev):
        push(src, dst, q_s.at[i], q_r.at[i], dev).start()

    def score_step(n):
        if n == 0:
            q_push(0, qb.at[1 - c], rq, {"states": core})
        elif n == 1:
            landed(rq, q_r.at[0])
            qy[...] = qb[c] + rq[...]
            for d in range(1, 4):
                q2 = (q + d) % 4
                q_push(1, qy.at[pl.ds(gray(q2) * 4, 4)], ry.at[d - 1], {"states": at(p, q2)})
        elif n == 2:
            landed(ry, q_r.at[1])
            qx[...] = qy[pl.ds(gray(q) * 4, 4)] + ry[0] + ry[1] + ry[2]
            for d in range(1, 4):
                p2 = (p + d) % 4
                q_push(2, qx.at[pl.ds(gray(p2), 1)], rx.at[d - 1], {"states": at(p2, q)})
        elif n == 3:
            landed(rx, q_r.at[2])
            q1[...] = qx[pl.ds(gray(p), 1)] + rx[0] + rx[1] + rx[2]
            for d in range(1, 4):
                q_push(3, q1, rh.at[d - 1], {"frames": (hi + d) % 4})
        else:
            landed(rh, q_r.at[3])
            quad = q1[0] + rh[0, 0] + rh[1, 0] + rh[2, 0]
            w_sum = jnp.sum(w_in[...].astype(BF16).astype(F32), axis=0, keepdims=True)
            for f in range(2):
                score_ref[f : f + 1, :] = -0.5 * quad[f : f + 1, :] / (D * w_sum[:, f * 128 : (f + 1) * 128])

    def outputs_here():
        landed(out.at[:, 0 : 32 * ROWS], o_c.at[0])
        landed(tb, l_s.at[0])

    def codes_start():
        gf.start(range(4))
        gf.start_core()

    do = {"G0": codes_start, "occ": occupancy, "OC": outputs_here}
    for h in range(5):
        if h:
            do[f"G{h}"] = lambda h=h: g_hop(h)
        do[f"GC{h}"] = lambda h=h: g_core(h)
        masks, n = HOPS[h], len(HOPS[h])
        pieces = (("", masks),) if n == 1 else (("0", masks[: n // 2]), ("1", masks[n // 2 :]))
        for tag, some in pieces:
            do[f"bo{h}{tag}"] = lambda some=some: build_all(c, slot[0], some)
            do[f"bc{h}{tag}"] = lambda some=some: build_all(1 - c, other[0], some)
    for e in range(2):
        do[f"Xs{e}a"] = lambda e=e: x_start(e, (0, 1))
        do[f"Xs{e}b"] = lambda e=e: x_start(e, (2, 3))
        do[f"XCs{e}"] = lambda e=e: x_start_core(e)
        for i in range(6):
            do[f"x{e}g{i}"] = lambda e=e, i=i: x_group(e, i)
            do[f"o{e}g{i}"] = lambda e=e, i=i: o_group(e, i)
            do[f"t{e}g{i}"] = lambda e=e, i=i: t_group(e, i)
        for i in range(3):
            do[f"XC{e}{i}"] = lambda e=e, i=i: x_core(e, i)
            do[f"U{e}{i}"] = lambda e=e, i=i: u_group(e, i)
        for mask in (0, 4, 8, 12):
            do[f"mo{mask}e{e}"] = lambda e=e, mask=mask: own_moments(mask, e)
            do[f"mc{mask}e{e}"] = lambda e=e, mask=mask: core_moments(mask, e)
        do[f"A{e}"] = lambda e=e: acc_send(e)
        do[f"AW{e}"] = lambda e=e: update(e)
        do[f"TW{e}"] = lambda e=e: table(e)
        for n in range(8):
            do[f"R{e}{n}"] = lambda e=e, n=n: rescore(e, n)
    for n in range(5):
        do[f"Q{n}"] = lambda n=n: score_step(n)

    with jax.named_scope("a0_barrier"):
        pl.semaphore_wait(barrier, 11)
    for n, name in enumerate(ORDER):
        with jax.named_scope(f"s{n:03d}_{name}"):
            do[name]()

    landed(g.at[0:31], g_s.at[0])
    landed(xs.at[:, :, 0:1984, 0:W], x_s.at[0])
    landed(out.at[:, 0 : 2 * (31 * OWN + 31 * LATE + 31 * (OWN - LATE))], o_s.at[0])
    landed(oc, oc_s.at[0])
    landed(racc, acc_s.at[0])
    landed(tb.at[:, :, 0:OWN], tb_s.at[0])
    landed(rq, q_s.at[0])
    landed(ry, q_s.at[1])
    landed(rx, q_s.at[2])
    landed(rh, q_s.at[3])


def write_kernel(both, score, means, precs, out_score, sems):
    n = means.shape[0] // PIECES
    copies = [
        pltpu.make_async_copy(both.at[a, i * n : (i + 1) * n], ref.at[i * n : (i + 1) * n], sems.at[a, i])
        for i in range(PIECES)
        for a, ref in enumerate((means, precs))
    ]
    copies.append(pltpu.make_async_copy(score, out_score, sems.at[2, 0]))
    for cp in copies:
        cp.start()
    for cp in copies:
        cp.wait()


def per_device(features, state_ids, weights):
    hbm = pl.BlockSpec(memory_space=pltpu.HBM)
    place = pl.BlockSpec(memory_space=pl.ANY)
    vm = pl.BlockSpec(memory_space=pltpu.VMEM)
    dma = pltpu.SemaphoreType.DMA
    states = 64 * ROWS
    both, score = pl.pallas_call(
        kernel,
        out_shape=(
            pltpu.VMEM((2, states, W), BF16),
            pltpu.VMEM((2, 128), F32),
        ),
        in_specs=[hbm] * 3,
        out_specs=(place, vm),
        scratch_shapes=[
            pltpu.VMEM((256, W), BF16),
            pltpu.VMEM((32, 256), I32),
            pltpu.VMEM((32, 256), F32),
            pltpu.VMEM((2, 2, 2048, 2 * W), BF16),
            pltpu.VMEM((32, 64, 256), I16),
            pltpu.VMEM((2, 2, 2 * ROWS, 2048), BF16),
            pltpu.VMEM((2, 2 * ROWS, W), F32),
            pltpu.VMEM((2, 2, OWN, W), F32),
            pltpu.VMEM((2 * ROWS, 128), F32),
            pltpu.VMEM((8, 256), F32),
            pltpu.VMEM((8, 256), F32),
            pltpu.VMEM((256, 128), F32),
            pltpu.VMEM((2, 2, ROWS, W), BF16),
            pltpu.VMEM((2, 2 * ROWS, W), BF16),
            pltpu.VMEM((2 * ROWS, 128), F32),
            pltpu.VMEM((2, 16, 2, 128), F32),
            pltpu.VMEM((16, 2, 128), F32),
            pltpu.VMEM((16, 2, 128), F32),
            pltpu.VMEM((3, 4, 2, 128), F32),
            pltpu.VMEM((4, 2, 128), F32),
            pltpu.VMEM((3, 1, 2, 128), F32),
            pltpu.VMEM((1, 2, 128), F32),
            pltpu.VMEM((3, 1, 2, 128), F32),
            dma((3,)),
            dma((1,)), dma((4,)), dma((5,)),
            dma((1,)), dma((2, 6)), dma((2, 3)),
            dma((1,)), dma((2, 6)), dma((2, 6)), dma((2, 3)), dma((1,)),
            dma((1,)), dma((2,)),
            dma((1,)), dma((2,)),
            dma((1,)), dma((1,)),
            dma((1,)),
            dma((4,)), dma((4,)),
        ],
        compiler_params=pltpu.CompilerParams(
            collective_id=0, has_side_effects=True, vmem_limit_bytes=40 << 20
        ),
        name="fused",
    )(*[pltpu.with_memory_space_constraint(a, pltpu.HBM) for a in (features, state_ids.T, weights.T)])
    means, precs, score = pl.pallas_call(
        write_kernel,
        out_shape=(
            jax.ShapeDtypeStruct((states, W), BF16),
            jax.ShapeDtypeStruct((states, W), BF16),
            jax.ShapeDtypeStruct((2, 128), F32),
        ),
        in_specs=[place] * 2,
        out_specs=(hbm,) * 3,
        scratch_shapes=[dma((3, PIECES))],
        compiler_params=pltpu.CompilerParams(vmem_limit_bytes=4 << 20),
        name="write",
    )(*[pltpu.with_memory_space_constraint(a, pltpu.VMEM) for a in (both, score)])
    return means, precs, score.reshape(-1)


def solution(mesh):
    return jax.shard_map(
        per_device,
        mesh=mesh,
        in_specs=(P("states", "frames"), P("states", None), P("states", None)),
        out_specs=(P(None, "frames"), P(None, "frames"), P("states")),
        check_vma=False,
    )
```
